256 devices in a mesh: grp: 4 (over x), tile: 64 (over y, z, core).
Axes of the slice: x: 4, y: 4, z: 8, core: 2. Of those that a mesh axis runs over, the one named last changes fastest.
Arguments:
- temp: bfloat16 [48, 64, 16384], P(None, 'grp', 'tile'), may hold values from -6 to 6
- humid: bfloat16 [48, 64, 16384], P(None, 'grp', 'tile'), may hold values from -5 to 5
- parent: int32 [64, 16384], P('grp', 'tile'), may hold values from 0 to 65535, as said below
- kabs: float32 [112, 48], replicated, may hold values from 0.003 to 1
- planck: float32 [112], replicated, may hold values from 0.5 to 2
- top_flux: float32 [112], replicated, may hold values from 0 to 2
Outputs:
- temp_next: bfloat16 [48, 64, 16384], P(None, 'grp', 'tile')
The draws below stay inside these ranges and needn't reach their ends.
Inputs may be any that keep to these rules, and one draw needn't show every extreme that they name: parent // 1024 is the tile index, in the same region, of the device owning that parent column; the fine cells of one device name any one owner at most 128 times.
All inputs are finite; a program needn't handle non-finite values.
Results may differ from the reference program's by a relative error of at most 0.005.
Values may be sent and summed in bfloat16 or wider, within the bound.
No kernel may reach another device: no remote copies, remote signals or barrier semaphores. Data moves between devices by JAX's collectives and lax.ppermute only.
A program may use at most 64 MiB of HBM per device.

```python
import math
import jax
import jax.numpy as jnp
from jax import lax

NLEV = 48
G = 112
FR = 16
FCOL = 256
CC = 1024
NCO = 65536
NY = 64
NX = 16384
N_GRP = 4
N_TILE = 64


def draw_parent(key, part):
    fine = FR * FCOL
    assigned_slots = 2 * fine
    capacity_limit = assigned_slots // N_TILE
    owned = fine // 4
    keys = jax.random.split(jax.random.fold_in(key, 17), 4)
    rank_keys = jax.random.split(keys[0], N_GRP)
    hot_rank = jax.vmap(lambda k: jax.random.permutation(k, N_TILE))(rank_keys)
    busiest_flag = (hot_rank < max(N_TILE // 4, 1)).astype(jnp.int32)
    random_jitter = jax.random.randint(keys[1], (N_GRP, N_TILE, assigned_slots), 0, 512)
    slot_numbers = jnp.arange(assigned_slots, dtype=jnp.int32)
    extra_priority = busiest_flag[:, slot_numbers // capacity_limit]
    ranking_score = (random_jitter + 512 * extra_priority[:, None, :]) * assigned_slots + slot_numbers[None, None, :]
    unused, chosen = lax.top_k(ranking_score, fine)
    chosen = jax.random.permutation(keys[2], chosen, axis=2, independent=True)
    owner = chosen // capacity_limit
    local = jax.random.randint(keys[3], (N_GRP, N_TILE, fine), 0, owned)
    parent = (owner * owned + local).astype(jnp.int32)
    parent = parent.reshape(N_GRP, N_TILE, FR, FCOL)
    return jnp.transpose(parent, (0, 2, 1, 3)).reshape(N_GRP * FR, N_TILE * FCOL)


def block_levels(own_key, shape, cuts, smallest, high):
    loudness = 1.0
    for dim, shards_of in cuts:
        heights = jax.random.uniform(jax.random.fold_in(jax.random.fold_in(own_key, 6), dim), (shards_of,), jnp.float32, smallest / len(cuts), high / len(cuts))
        loudness = loudness * jnp.repeat(jnp.exp(heights), shape[dim] // shards_of).reshape((-1,) + (1,) * (len(shape) - 1 - dim))
    return loudness


def gaussian(key, extent, width, limit, cuts=(), kind=jnp.bfloat16):
    drawn = width * jax.random.normal(key, extent, jnp.float32)
    if cuts:
        drawn = drawn * block_levels(key, extent, cuts, -0.22, 0.18)
    return jnp.clip(drawn, -limit, limit).astype(kind)


def setup_inputs(seed: int = 0) -> dict:
    seeds = jax.random.split(jax.random.key(seed), 7)
    return {
        "temp": gaussian(seeds[0], (NLEV, NY, NX), 1.0, 6.0, ((1, 4), (2, 64))),
        "humid": gaussian(seeds[1], (NLEV, NY, NX), 1.0, 5.0, ((1, 4), (2, 64))),
        "parent": draw_parent(jax.random.fold_in(seeds[6], 71), 0),
        "kabs": jnp.clip(jnp.exp(jax.random.uniform(seeds[3], (G, NLEV), jnp.float32, math.log(0.003), math.log(1.0))), 0.003, 1.0),
        "planck": jnp.clip(jnp.exp(jax.random.uniform(seeds[4], (G,), jnp.float32, math.log(0.5), math.log(2.0))), 0.5, 2.0),
        "top_flux": jnp.clip(jax.random.uniform(seeds[5], (G,), jnp.float32, 0.0, 2.0), 0.0, 2.0),
    }


def recur(coef, source, init):
    levels = coef.shape[0]
    blocks = levels // 8
    rest = coef.shape[1:]
    coef4 = coef.reshape((blocks, 8) + rest)
    source4 = source.reshape((blocks, 8) + rest)
    prod_list = []
    part_list = []
    prod_now = jnp.ones((blocks,) + rest, jnp.float32)
    part_now = jnp.zeros((blocks,) + rest, jnp.float32)
    for inner in range(8):
        prod_now = coef4[:, inner] * prod_now
        part_now = coef4[:, inner] * part_now + source4[:, inner]
        prod_list.append(prod_now)
        part_list.append(part_now)
    starts = []
    carry = init
    for outer in range(blocks):
        starts.append(carry)
        carry = prod_list[7][outer] * carry + part_list[7][outer]
    start = jnp.stack(starts, 0)
    result = jnp.stack([prod_list[j] * start + part_list[j] for j in range(8)], 1)
    return result.reshape((levels,) + rest)


def radiate(tc, hc, kabs, planck, top_flux):
    levels, count = tc.shape
    kblk = kabs.reshape(-1, 16, levels)
    pblk = planck.reshape(-1, 16)
    tblk = top_flux.reshape(-1, 16)
    absorb = jnp.exp(0.5 * hc)[:, None, :]
    emit = jnp.exp(0.25 * tc)[:, None, :]

    def one_block(items):
        k_blk, p_blk, t_blk = items
        tau = jnp.transpose(k_blk)[:, :, None] * absorb
        trans = jnp.exp(-tau)
        source = p_blk[None, :, None] * emit * (1.0 - trans)
        top = jnp.broadcast_to(t_blk[:, None], (16, count)).astype(jnp.float32)
        down = recur(trans, source, top)
        up = recur(trans[::-1], source[::-1], 0.3 * down[-1])[::-1]
        net = down - up
        top_net = top - up[0]
        before = jnp.concatenate([top_net[None], net[:-1]], 0)
        return jnp.sum(before - net, axis=1)

    parts = lax.map(one_block, (kblk, pblk, tblk))
    return jnp.sum(parts, axis=0) * (levels / kabs.shape[0])


def laplace(field):
    value = field.astype(jnp.float32)
    return (jnp.roll(value, 1, 1) + jnp.roll(value, -1, 1) + jnp.roll(value, 1, 2) + jnp.roll(value, -1, 2) - 4.0 * value)


def reference(temp, humid, parent, kabs, planck, top_flux):
    levels = temp.shape[0]
    first = (temp.astype(jnp.float32) + 0.2 * laplace(temp)).astype(jnp.bfloat16)
    region = (jnp.arange(NY) // FR).astype(jnp.int32)
    global_id = (region[:, None] * NCO + parent).reshape(-1)
    total = N_GRP * NCO
    values = jnp.concatenate([temp.reshape(levels, -1), humid.reshape(levels, -1)], 0).astype(jnp.float32)
    sums = jax.ops.segment_sum(jnp.transpose(values), global_id, num_segments=total)
    counts = jax.ops.segment_sum(jnp.ones(global_id.shape, jnp.float32), global_id, num_segments=total)
    means = sums / jnp.maximum(counts, 1.0)[:, None]
    blocks = means.reshape(total // CC, CC, 2 * levels)

    def per_owner(block):
        tc = jnp.transpose(block[:, :levels])
        hc = jnp.transpose(block[:, levels:])
        return radiate(tc, hc, kabs, planck, top_flux)

    heat = lax.map(per_owner, blocks)
    heat_c = jnp.transpose(heat, (1, 0, 2)).reshape(levels, total).astype(jnp.bfloat16)
    hmean = jnp.transpose(means[:, levels:]).astype(jnp.bfloat16)
    heat_f = heat_c[:, global_id].astype(jnp.float32) + 0.5 * (humid.reshape(levels, -1).astype(jnp.float32) - hmean[:, global_id].astype(jnp.float32))
    second = (first.astype(jnp.float32) + 0.5 * heat_f.reshape(temp.shape)).astype(jnp.bfloat16)
    return (second.astype(jnp.float32) + 0.2 * laplace(second)).astype(jnp.bfloat16)
```

```python
import functools
import jax
import jax.numpy as jnp
from jax import lax
from jax.experimental import pallas as pl
from jax.experimental.pallas import tpu as pltpu
from jax.sharding import PartitionSpec as P

F32 = jnp.float32
BF16 = jnp.bfloat16
LEV = 48
G = 112
ROWS = 16
COLS = 256
OWNED = 1024
TILES = 64
CAP = 128
PAIRS = TILES // 2
BLK_ROW = 96
LOW_ROW = 97
ONE_ROW = 98
SEND = 104
WIDE = 112
GB = 8
VMEM = 56 * 1024 * 1024


def params():
    return pltpu.CompilerParams(vmem_limit_bytes=VMEM)


def whole(n):
    return [pl.BlockSpec(memory_space=pltpu.VMEM)] * n


def pack_kernel(temp_ref, humid_ref, parent_ref, send_ref, slot_ref, x_ref, b_ref, pair_ref):
    sub = lax.broadcasted_iota(jnp.int32, (COLS, COLS), 0)
    lane = lax.broadcasted_iota(jnp.int32, (COLS, COLS), 1)
    before = (sub < lane).astype(BF16)
    ones = jnp.ones((COLS, COLS), BF16)
    sub64 = lax.broadcasted_iota(jnp.int32, (TILES, COLS), 0)
    carry = jnp.zeros((TILES, COLS), F32)
    sub16 = lax.broadcasted_iota(jnp.int32, (16, COLS), 0)
    for r in range(ROWS):
        parent = parent_ref[r : r + 1, :]
        owner = parent // OWNED
        local = parent % OWNED
        hit = jnp.where(owner == sub64, 1.0, 0.0).astype(F32)
        hit16 = hit.astype(BF16)
        rank = jnp.dot(hit16, before, preferred_element_type=F32) + carry
        carry = carry + jnp.dot(hit16, ones, preferred_element_type=F32)
        position = jnp.sum(hit * rank, axis=0, keepdims=True).astype(jnp.int32)
        slot = owner * CAP + position
        slot_ref[r : r + 1, :] = slot
        cols = pl.ds(r * COLS, COLS)
        x_ref[0:LEV, cols] = temp_ref[r]
        x_ref[LEV : 2 * LEV, cols] = humid_ref[r]
        blk = (local // 256 + 1).astype(F32)
        low = (local % 256).astype(F32)
        extra = jnp.where(sub16 == 0, blk, jnp.where(sub16 == 1, low, jnp.where(sub16 == 2, 1.0, 0.0)))
        x_ref[2 * LEV : WIDE, cols] = extra.astype(BF16)
        onehot = jnp.where((slot % 256) == sub, 1.0, 0.0).astype(F32)
        b_ref[cols, :] = onehot.T.astype(BF16)
        pair_ref[:, cols] = jnp.broadcast_to((slot // 256).astype(F32), (16, COLS)).astype(BF16)

    def one_pair(p, _):
        mask = pair_ref[...] == p.astype(F32).astype(BF16)
        values = x_ref[...].reshape(WIDE // 16, 16, ROWS * COLS)
        chosen = jnp.where(mask[None], values, jnp.zeros_like(values)).reshape(WIDE, ROWS * COLS)
        moved = jnp.dot(chosen, b_ref[...], preferred_element_type=F32)
        moved = moved[0:SEND].astype(BF16)
        send_ref[2 * p] = moved[:, 0:CAP]
        send_ref[2 * p + 1] = moved[:, CAP : 2 * CAP]
        return 0

    lax.fori_loop(0, PAIRS, one_pair, 0)


def pack(temp_t, humid_t, parent):
    return pl.pallas_call(
        pack_kernel,
        out_shape=(
            jax.ShapeDtypeStruct((TILES, SEND, CAP), BF16),
            jax.ShapeDtypeStruct((ROWS, COLS), jnp.int32),
        ),
        in_specs=whole(3),
        out_specs=tuple(whole(2)),
        scratch_shapes=[
            pltpu.VMEM((WIDE, ROWS * COLS), BF16),
            pltpu.VMEM((ROWS * COLS, COLS), BF16),
            pltpu.VMEM((16, ROWS * COLS), BF16),
        ],
        compiler_params=params(),
    )(temp_t, humid_t, parent)


def owner_kernel(recv_ref, kabs_ref, planck_ref, top_ref, out_ref,
                 b_ref, absorb_ref, emit_ref, hmean_ref, net_ref, trans_ref, sum_ref, q_ref):
    sub = lax.broadcasted_iota(jnp.int32, (256, CAP), 0).astype(F32)

    sum_ref[...] = jnp.zeros_like(sum_ref)

    def one_pair(p, _):
        lhs = []
        for h in range(2):
            got = recv_ref[2 * p + h].astype(F32)
            low = got[LOW_ROW : LOW_ROW + 1]
            blk = got[BLK_ROW : BLK_ROW + 1]
            b_ref[p, :, h * CAP : (h + 1) * CAP] = jnp.where(low == sub, 1.0, 0.0).astype(BF16)
            lhs.append(
                jnp.concatenate(
                    [jnp.where(blk == float(b + 1), got, 0.0).astype(BF16) for b in range(4)], axis=0
                )
            )
        both = jnp.concatenate(lhs, axis=1)
        sum_ref[...] += lax.dot_general(
            both, b_ref[p], (((1,), (1,)), ((), ())), preferred_element_type=F32
        )
        return 0

    lax.fori_loop(0, PAIRS, one_pair, 0)

    rows = []
    for b in range(4):
        for h in range(2):
            rows.append(sum_ref[b * SEND + ONE_ROW : b * SEND + ONE_ROW + 1, h * CAP : (h + 1) * CAP])
    inv = 1.0 / jnp.maximum(jnp.concatenate(rows, axis=0), 1.0)
    for b in range(4):
        for h in range(2):
            lanes = slice(h * CAP, (h + 1) * CAP)
            emit_ref[:, 2 * b + h, :] = sum_ref[b * SEND : b * SEND + LEV, lanes]
            hmean_ref[:, 2 * b + h, :] = sum_ref[b * SEND + LEV : b * SEND + 2 * LEV, lanes]
    hc = hmean_ref[...] * inv[None]
    absorb_ref[...] = jnp.exp(0.5 * hc)
    emit_ref[...] = jnp.exp(0.25 * (emit_ref[...] * inv[None]))
    hmean_ref[...] = hc
    net_ref[...] = jnp.zeros_like(net_ref)

    def one_block(gb, top_sum):
        first = gb * GB
        tops = [top_ref[first + j] for j in range(GB)]
        planck = [planck_ref[first + j] for j in range(GB)]

        def down_step(k, state):
            absorb = absorb_ref[k]
            emit = emit_ref[k]
            new = []
            total = None
            for j in range(GB):
                t = jnp.exp(absorb * (-kabs_ref[first + j, k]))
                trans_ref[k, j] = t
                s = emit * planck[j]
                d = s + t * (state[j] - s)
                new.append(d)
                total = d if total is None else total + d
            net_ref[k] += total
            return tuple(new)

        start = tuple(jnp.full((8, 128), tops[j], F32) for j in range(GB))
        down = lax.fori_loop(0, LEV, down_step, start, unroll=4)

        def up_step(i, state):
            k = LEV - 1 - i
            emit = emit_ref[k]
            new = []
            total = None
            for j in range(GB):
                s = emit * planck[j]
                u = s + trans_ref[k, j] * (state[j] - s)
                new.append(u)
                total = u if total is None else total + u
            net_ref[k] -= total
            return tuple(new)

        up = lax.fori_loop(0, LEV, up_step, tuple(0.3 * d for d in down), unroll=4)
        for j in range(GB):
            top_sum = top_sum + (tops[j] - up[j])
        return top_sum

    top_net = lax.fori_loop(0, G // GB, one_block, jnp.zeros((8, 128), F32))
    net = net_ref[...]
    prev = jnp.concatenate([top_net[None], net[:-1]], axis=0)
    heat = ((prev - net) * (LEV / G)).astype(BF16).astype(F32)
    hm = hmean_ref[...].astype(BF16).astype(F32)
    net_ref[...] = heat - 0.5 * hm
    for b in range(4):
        for h in range(2):
            q_ref[b * LEV : (b + 1) * LEV, h * CAP : (h + 1) * CAP] = net_ref[:, 2 * b + h, :].astype(BF16)

    def answer(p, _):
        both = jnp.dot(q_ref[...], b_ref[p], preferred_element_type=F32)
        for h in range(2):
            lanes = slice(h * CAP, (h + 1) * CAP)
            blk = recv_ref[2 * p + h, BLK_ROW : BLK_ROW + 8, :].astype(F32)[0:1]
            got = jnp.zeros((LEV, CAP), F32)
            for b in range(4):
                got = jnp.where(blk == float(b + 1), both[b * LEV : (b + 1) * LEV, lanes], got)
            out_ref[2 * p + h] = got.astype(BF16)
        return 0

    lax.fori_loop(0, PAIRS, answer, 0)


def owner_step(recv, kabs, planck, top_flux):
    smem = pl.BlockSpec(memory_space=pltpu.SMEM)
    return pl.pallas_call(
        owner_kernel,
        out_shape=jax.ShapeDtypeStruct((TILES, LEV, CAP), BF16),
        in_specs=whole(1) + [smem, smem, smem],
        out_specs=whole(1)[0],
        scratch_shapes=[
            pltpu.VMEM((PAIRS, 256, 256), BF16),
            pltpu.VMEM((LEV, 8, 128), F32),
            pltpu.VMEM((LEV, 8, 128), F32),
            pltpu.VMEM((LEV, 8, 128), F32),
            pltpu.VMEM((LEV, 8, 128), F32),
            pltpu.VMEM((LEV, GB, 8, 128), F32),
            pltpu.VMEM((4 * SEND, 256), F32),
            pltpu.VMEM((4 * LEV, 256), BF16),
        ],
        compiler_params=params(),
    )(recv, kabs, planck, top_flux)


def stencil_row(value, above, below, left, right):
    lane = lax.broadcasted_iota(jnp.int32, value.shape, 1)
    west = jnp.where(lane == 0, left, pltpu.roll(value, 1, axis=1))
    east = jnp.where(lane == COLS - 1, right, pltpu.roll(value, COLS - 1, axis=1))
    return value + 0.2 * (above + below + west + east - 4.0 * value)


def stencil_kernel(field_ref, above_ref, below_ref, left_ref, right_ref, out_ref):
    left = left_ref[...].astype(F32)
    right = right_ref[...].astype(F32)
    for r in range(ROWS):
        value = field_ref[r].astype(F32)
        above = (above_ref[...] if r == 0 else field_ref[r - 1]).astype(F32)
        below = (below_ref[...] if r == ROWS - 1 else field_ref[r + 1]).astype(F32)
        out_ref[r] = stencil_row(
            value, above, below, left[:, r : r + 1], right[:, r : r + 1]
        ).astype(BF16)


def stencil(field, halo):
    return pl.pallas_call(
        stencil_kernel,
        out_shape=jax.ShapeDtypeStruct((ROWS, LEV, COLS), BF16),
        in_specs=whole(5),
        out_specs=whole(1)[0],
        compiler_params=params(),
    )(field, *halo)


def unpack_kernel(ret_ref, slot_ref, first_ref, humid_ref, second_ref, left_ref, right_ref, r_ref):
    sub = lax.broadcasted_iota(jnp.int32, (256, COLS), 0)
    lane = lax.broadcasted_iota(jnp.int32, (LEV, 128), 1)
    for p in range(PAIRS):
        for h in range(2):
            r_ref[p * LEV : (p + 1) * LEV, h * CAP : (h + 1) * CAP] = ret_ref[2 * p + h]
    left_ref[...] = jnp.zeros_like(left_ref)
    right_ref[...] = jnp.zeros_like(right_ref)

    def one_row(r, _):
        slot = slot_ref[pl.ds(r, 1), :]
        onehot = jnp.where((slot % 256) == sub, 1.0, 0.0).astype(BF16)
        pair = slot // 256
        moved = jnp.dot(r_ref[...], onehot, preferred_element_type=F32)
        q = jnp.zeros((LEV, COLS), F32)
        for p in range(PAIRS):
            q = jnp.where(pair == p, moved[p * LEV : (p + 1) * LEV], q)
        heat = q + 0.5 * humid_ref[r].astype(F32)
        second = (first_ref[r].astype(F32) + 0.5 * heat).astype(BF16)
        second_ref[r] = second
        second = second.astype(F32)
        left_ref[...] = jnp.where(lane == r, second[:, 0:1], left_ref[...].astype(F32)).astype(BF16)
        right_ref[...] = jnp.where(lane == r, second[:, COLS - 1 : COLS], right_ref[...].astype(F32)).astype(BF16)
        return 0

    lax.fori_loop(0, ROWS, one_row, 0)


def unpack(ret, slot, first, humid_t):
    edge = jax.ShapeDtypeStruct((LEV, 128), BF16)
    return pl.pallas_call(
        unpack_kernel,
        out_shape=(jax.ShapeDtypeStruct((ROWS, LEV, COLS), BF16), edge, edge),
        in_specs=whole(4),
        out_specs=tuple(whole(3)),
        scratch_shapes=[pltpu.VMEM((PAIRS * LEV, 256), BF16)],
        compiler_params=params(),
    )(ret, slot, first, humid_t)


def exchange(top, bottom, left, right):
    grp = lax.axis_size("grp")
    tile = lax.axis_size("tile")
    up = [(i, (i + 1) % grp) for i in range(grp)]
    along = [(i, (i + 1) % tile) for i in range(tile)]
    above = lax.ppermute(bottom, "grp", up)
    below = lax.ppermute(top, "grp", [(b, a) for a, b in up])
    west = lax.ppermute(right, "tile", along)
    east = lax.ppermute(left, "tile", [(b, a) for a, b in along])
    return above, below, west, east


def edge_columns(column):
    return jnp.pad(jnp.transpose(column), ((0, 0), (0, 128 - ROWS)))


def on_device(temp, humid, parent, kabs, planck, top_flux):
    temp_t = jnp.transpose(temp, (1, 0, 2))
    humid_t = jnp.transpose(humid, (1, 0, 2))
    halo = exchange(
        temp_t[0], temp_t[ROWS - 1], edge_columns(temp_t[:, :, 0]), edge_columns(temp_t[:, :, COLS - 1])
    )
    send, slot = pack(temp_t, humid_t, parent)
    recv = lax.all_to_all(send, "tile", split_axis=0, concat_axis=0, tiled=True)
    first = stencil(temp_t, halo)
    answer = owner_step(recv, kabs, planck, top_flux)
    ret = lax.all_to_all(answer, "tile", split_axis=0, concat_axis=0, tiled=True)
    second, left, right = unpack(ret, slot, first, humid_t)
    halo2 = exchange(second[0], second[ROWS - 1], left, right)
    return jnp.transpose(stencil(second, halo2), (1, 0, 2))


def solution(mesh):
    placed = (P(None, "grp", "tile"), P(None, "grp", "tile"), P("grp", "tile"), P(), P(), P())
    return jax.shard_map(
        on_device, mesh=mesh, in_specs=placed, out_specs=P(None, "grp", "tile"), check_vma=False
    )
```

```python
import jax
import jax.numpy as jnp
from jax import lax
from jax.experimental import pallas as pl
from jax.experimental.pallas import tpu as pltpu
from jax.sharding import PartitionSpec as P

F32 = jnp.float32
BF16 = jnp.bfloat16
LEV = 48
G = 112
ROWS = 16
COLS = 256
CELLS = ROWS * COLS
OWNED = 1024
TILES = 64
CAP = 128
PAIRS = TILES // 2
BLK_ROW = 96
ONE_ROW = 98
SEND = 104
WIDE = 112
GROUP = 8
GB = 4
LOG2E = 1.4426950408889634
VMEM = 56 * 1024 * 1024


def call(kernel, out_shape, operands, scratch=(), scalars=0):
    vmem = pl.BlockSpec(memory_space=pltpu.VMEM)
    smem = pl.BlockSpec(memory_space=pltpu.SMEM)
    many = isinstance(out_shape, tuple)
    return pl.pallas_call(
        kernel,
        out_shape=out_shape,
        in_specs=[vmem] * (len(operands) - scalars) + [smem] * scalars,
        out_specs=(vmem,) * len(out_shape) if many else vmem,
        scratch_shapes=list(scratch),
        compiler_params=pltpu.CompilerParams(vmem_limit_bytes=VMEM),
    )(*operands)


def pack_kernel(temp_ref, humid_ref, parent_ref, send_ref, slot_ref, t_ref, h_ref, x_ref, b_ref, pair_ref):
    t_ref[...] = temp_ref[...].astype(F32)
    h_ref[...] = humid_ref[...].astype(F32)
    sub = lax.broadcasted_iota(jnp.int32, (COLS, COLS), 0)
    lane = lax.broadcasted_iota(jnp.int32, (COLS, COLS), 1)
    before = (sub < lane).astype(BF16)
    ones = jnp.ones((COLS, COLS), BF16)
    sub64 = lax.broadcasted_iota(jnp.int32, (TILES, COLS), 0)
    sub16 = lax.broadcasted_iota(jnp.int32, (16, COLS), 0)
    parent = parent_ref[...]
    owner = parent // OWNED
    local = parent % OWNED
    blk = (local // 256 + 1).astype(F32)
    low = (local % 256).astype(F32)
    hits = [jnp.where(owner[r : r + 1] == sub64, 1.0, 0.0).astype(F32) for r in range(ROWS)]
    stacked = jnp.concatenate([h.astype(BF16) for h in hits], axis=0)
    ranks = jnp.dot(stacked, before, preferred_element_type=F32)
    totals = jnp.dot(stacked, ones, preferred_element_type=F32)
    carry = jnp.zeros((TILES, COLS), F32)
    position = []
    for r in range(ROWS):
        span = slice(r * TILES, (r + 1) * TILES)
        position.append(jnp.sum(hits[r] * (ranks[span] + carry), axis=0, keepdims=True))
        carry = carry + totals[span]
    slot = owner * CAP + jnp.concatenate(position, axis=0).astype(jnp.int32)
    slot_ref[...] = slot
    pair = (slot // 256).astype(F32)
    within = (slot % 256).astype(F32).T
    lane_f = lane.astype(F32)
    for r in range(ROWS):
        cols = slice(r * COLS, (r + 1) * COLS)
        x_ref[0:LEV, cols] = t_ref[:, r, :].astype(BF16)
        x_ref[LEV : 2 * LEV, cols] = h_ref[:, r, :].astype(BF16)
        extra = jnp.where(
            sub16 == 0, blk[r : r + 1], jnp.where(sub16 == 1, low[r : r + 1], jnp.where(sub16 == 2, 1.0, 0.0))
        )
        x_ref[2 * LEV : WIDE, cols] = extra.astype(BF16)
        b_ref[cols, :] = jnp.where(within[:, r : r + 1] == lane_f, 1.0, 0.0).astype(BF16)
        pair_ref[:, cols] = jnp.broadcast_to(pair[r : r + 1], (16, COLS)).astype(BF16)

    def one_group(step, _):
        values = x_ref[...].reshape(WIDE // 16, 16, CELLS)
        chosen = []
        for j in range(GROUP):
            mask = pair_ref[...] == (step * GROUP + j).astype(F32).astype(BF16)
            chosen.append(jnp.where(mask[None], values, jnp.zeros_like(values)).reshape(WIDE, CELLS))
        moved = jnp.dot(jnp.concatenate(chosen, axis=0), b_ref[...], preferred_element_type=F32)
        for j in range(GROUP):
            p = step * GROUP + j
            part = moved[j * WIDE : j * WIDE + SEND].astype(BF16)
            send_ref[2 * p] = part[:, 0:CAP]
            send_ref[2 * p + 1] = part[:, CAP : 2 * CAP]
        return 0

    lax.fori_loop(0, PAIRS // GROUP, one_group, 0)


def pack(temp, humid, parent):
    return call(
        pack_kernel,
        (
            jax.ShapeDtypeStruct((TILES, SEND, CAP), BF16),
            jax.ShapeDtypeStruct((ROWS, COLS), jnp.int32),
        ),
        (temp, humid, parent),
        [
            pltpu.VMEM((LEV, ROWS, COLS), F32),
            pltpu.VMEM((LEV, ROWS, COLS), F32),
            pltpu.VMEM((WIDE, CELLS), BF16),
            pltpu.VMEM((CELLS, COLS), BF16),
            pltpu.VMEM((16, CELLS), BF16),
        ],
    )


def owner_kernel(recv_ref, kabs_ref, planck_ref, top_ref, out_ref,
                 b_ref, absorb_ref, emit_ref, step_ref, hmean_ref, net_ref, trans_ref, sum_ref, q_ref):
    sub = lax.broadcasted_iota(jnp.int32, (256, CAP), 0).astype(F32)
    lane = lax.broadcasted_iota(jnp.int32, (CAP, 256), 1).astype(F32)
    lows = jnp.concatenate([recv_ref[s, BLK_ROW:SEND, :].astype(F32)[1:2] for s in range(TILES)], axis=0)
    low_cols = lows.T

    for first in range(0, TILES, 4):
        lhs = []
        rhs = []
        for s in range(first, first + 4):
            got = recv_ref[s]
            blk = jnp.broadcast_to(got[BLK_ROW:SEND].astype(F32)[0:1], (SEND, CAP)).astype(BF16)
            half = slice((s % 2) * CAP, (s % 2 + 1) * CAP)
            b_ref[s // 2, :, half] = jnp.where(lows[s : s + 1] == sub, 1.0, 0.0).astype(BF16)
            rhs.append(jnp.where(low_cols[:, s : s + 1] == lane, 1.0, 0.0).astype(BF16))
            zero = jnp.zeros_like(got)
            lhs.append(
                jnp.concatenate([jnp.where(blk == jnp.asarray(b + 1, BF16), got, zero) for b in range(4)], axis=0)
            )
        part = jnp.dot(
            jnp.concatenate(lhs, axis=1), jnp.concatenate(rhs, axis=0), preferred_element_type=F32
        )
        if first == 0:
            sum_ref[...] = part
        else:
            sum_ref[...] += part

    counts = []
    for b in range(4):
        for h in range(2):
            lanes = slice(h * CAP, (h + 1) * CAP)
            row = b * SEND + ONE_ROW
            counts.append(sum_ref[row : row + 1, lanes])
            emit_ref[:, 2 * b + h, :] = sum_ref[b * SEND : b * SEND + LEV, lanes]
            hmean_ref[:, 2 * b + h, :] = sum_ref[b * SEND + LEV : b * SEND + 2 * LEV, lanes]
    inv = 1.0 / jnp.maximum(jnp.concatenate(counts, axis=0), 1.0)
    hc = hmean_ref[...] * inv[None]
    absorb_ref[...] = jnp.exp(0.5 * hc)
    emit = jnp.exp(0.25 * (emit_ref[...] * inv[None]))
    emit_ref[...] = emit
    step_ref[0 : LEV - 1] = emit[1:LEV] - emit[0 : LEV - 1]
    hmean_ref[...] = hc
    net_ref[...] = jnp.zeros_like(net_ref)
    emit_top = emit_ref[0]
    emit_low = emit_ref[LEV - 1]

    def one_block(block, top_net):
        first = block * GB
        tops = [top_ref[first + j] for j in range(GB)]
        planck = [planck_ref[first + j] for j in range(GB)]
        state = [tops[j] - emit_top * planck[j] for j in range(GB)]
        for k in range(LEV):
            absorb = absorb_ref[k]
            total = None
            for j in range(GB):
                t = jnp.exp2(absorb * kabs_ref[first + j, k])
                trans_ref[k, j] = t
                state[j] = t * state[j]
                total = state[j] if total is None else total + state[j]
            net_ref[k] += total
            if k < LEV - 1:
                step = step_ref[k]
                state = [state[j] - step * planck[j] for j in range(GB)]
        state = [
            0.3 * (state[j] + emit_low * planck[j]) - emit_low * planck[j] for j in range(GB)
        ]
        for k in range(LEV - 1, -1, -1):
            total = None
            for j in range(GB):
                state[j] = trans_ref[k, j] * state[j]
                total = state[j] if total is None else total + state[j]
            net_ref[k] -= total
            if k > 0:
                step = step_ref[k - 1]
                state = [state[j] + step * planck[j] for j in range(GB)]
        for j in range(GB):
            top_net = top_net + (tops[j] - (state[j] + emit_top * planck[j]))
        return top_net

    top_net = lax.fori_loop(0, G // GB, one_block, jnp.zeros((8, 128), F32))
    net = net_ref[...]
    prev = jnp.concatenate([top_net[None], net[:-1]], axis=0)
    heat = ((prev - net) * (LEV / G)).astype(BF16).astype(F32)
    hm = hmean_ref[...].astype(BF16).astype(F32)
    net_ref[...] = heat - 0.5 * hm
    for b in range(4):
        for h in range(2):
            q_ref[b * LEV : (b + 1) * LEV, h * CAP : (h + 1) * CAP] = net_ref[:, 2 * b + h, :].astype(BF16)

    for p in range(PAIRS):
        both = jnp.dot(q_ref[...], b_ref[p], preferred_element_type=F32)
        for h in range(2):
            lanes = slice(h * CAP, (h + 1) * CAP)
            blk = recv_ref[2 * p + h, BLK_ROW:SEND, :].astype(F32)[0:1]
            got = jnp.zeros((LEV, CAP), F32)
            for b in range(4):
                got = jnp.where(blk == float(b + 1), both[b * LEV : (b + 1) * LEV, lanes], got)
            out_ref[2 * p + h] = got.astype(BF16)


def owner_step(recv, kabs, planck, top_flux):
    column = pltpu.VMEM((LEV, 8, 128), F32)
    return call(
        owner_kernel,
        jax.ShapeDtypeStruct((TILES, LEV, CAP), BF16),
        (recv, kabs * (-LOG2E), planck, top_flux),
        [
            pltpu.VMEM((PAIRS, 256, 256), BF16),
            column,
            column,
            column,
            column,
            column,
            pltpu.VMEM((LEV, GB, 8, 128), F32),
            pltpu.VMEM((4 * SEND, 256), F32),
            pltpu.VMEM((4 * LEV, 256), BF16),
        ],
        scalars=3,
    )


def gather_columns(row_of):
    first = row_of(0)
    lane = lax.broadcasted_iota(jnp.int32, (first.shape[0], 128), 1)
    kept = jnp.zeros((first.shape[0], 128), first.dtype)
    for r in range(ROWS):
        row = row_of(r)
        kept = jnp.where(lane == r, row[:, 0:1], kept)
        kept = jnp.where(lane == ROWS + r, row[:, COLS - 1 : COLS], kept)
    return kept


def split_columns(columns):
    return columns.astype(BF16), pltpu.roll(columns, 128 - ROWS, axis=1).astype(BF16)


def edge_shapes():
    row = jax.ShapeDtypeStruct((LEV, COLS), BF16)
    column = jax.ShapeDtypeStruct((LEV, 128), BF16)
    return row, row, column, column


def edges_kernel(temp_ref, top_ref, bottom_ref, left_ref, right_ref, t_ref):
    t_ref[...] = temp_ref[...].astype(F32)
    top_ref[...] = t_ref[:, 0, :].astype(BF16)
    bottom_ref[...] = t_ref[:, ROWS - 1, :].astype(BF16)
    left_ref[...], right_ref[...] = split_columns(gather_columns(lambda r: t_ref[:, r, :]))


def edges(temp):
    return call(edges_kernel, edge_shapes(), (temp,), [pltpu.VMEM((LEV, ROWS, COLS), F32)])


def stencil_row(value, above, below, left, right):
    lane = lax.broadcasted_iota(jnp.int32, value.shape, 1)
    west = jnp.where(lane == 0, left, pltpu.roll(value, 1, axis=1))
    east = jnp.where(lane == COLS - 1, right, pltpu.roll(value, COLS - 1, axis=1))
    return value + 0.2 * (above + below + west + east - 4.0 * value)


def stencil_rows(row_of, above_ref, below_ref, left_ref, right_ref):
    left = left_ref[...].astype(F32)
    right = right_ref[...].astype(F32)
    above = above_ref[...].astype(F32)
    value = row_of(0)
    for r in range(ROWS):
        below = row_of(r + 1) if r < ROWS - 1 else below_ref[...].astype(F32)
        yield r, stencil_row(value, above, below, left[:, r : r + 1], right[:, r : r + 1])
        above, value = value, below


def base_kernel(temp_ref, humid_ref, slot_ref, above_ref, below_ref, left_ref, right_ref,
                base_ref, base_cols_ref, slot_cols_ref, t_ref, h_ref):
    t_ref[...] = temp_ref[...].astype(F32)
    h_ref[...] = humid_ref[...].astype(F32)
    for r, first in stencil_rows(lambda r: t_ref[:, r, :], above_ref, below_ref, left_ref, right_ref):
        base_ref[r] = first.astype(BF16).astype(F32) + 0.25 * h_ref[:, r, :]
    base_cols_ref[...] = gather_columns(lambda r: base_ref[r])
    slot = slot_ref[...]
    slots = gather_columns(lambda r: slot[r : r + 1])
    slot_cols_ref[...] = jnp.broadcast_to(slots, (8, 128))


def base_step(temp, humid, slot, halo):
    return call(
        base_kernel,
        (
            jax.ShapeDtypeStruct((ROWS, LEV, COLS), F32),
            jax.ShapeDtypeStruct((LEV, 128), F32),
            jax.ShapeDtypeStruct((8, 128), jnp.int32),
        ),
        (temp, humid, slot, *halo),
        [pltpu.VMEM((LEV, ROWS, COLS), F32), pltpu.VMEM((LEV, ROWS, COLS), F32)],
    )


def in_pairs(ret_ref, r_ref):
    for p in range(PAIRS):
        for h in range(2):
            r_ref[p * LEV : (p + 1) * LEV, h * CAP : (h + 1) * CAP] = ret_ref[2 * p + h]


def picked(r_ref, slot):
    count = slot.shape[1]
    sub = lax.broadcasted_iota(jnp.int32, (256, count), 0)
    onehot = jnp.where((slot % 256) == sub, 1.0, 0.0).astype(BF16)
    pair = slot // 256
    moved = jnp.dot(r_ref[...], onehot, preferred_element_type=F32)
    q = jnp.zeros((LEV, count), F32)
    for p in range(PAIRS):
        q = jnp.where(pair == p, moved[p * LEV : (p + 1) * LEV], q)
    return q


def rim_kernel(ret_ref, slot_ref, slot_cols_ref, base_top_ref, base_bottom_ref, base_cols_ref,
               top_ref, bottom_ref, left_ref, right_ref, r_ref):
    in_pairs(ret_ref, r_ref)
    slot = jnp.concatenate(
        [slot_ref[0:1, :], slot_ref[ROWS - 1 : ROWS, :], slot_cols_ref[0:1, :]], axis=1
    )
    q = 0.5 * picked(r_ref, slot)
    top_ref[...] = (base_top_ref[0] + q[:, 0:COLS]).astype(BF16)
    bottom_ref[...] = (base_bottom_ref[0] + q[:, COLS : 2 * COLS]).astype(BF16)
    left_ref[...], right_ref[...] = split_columns(base_cols_ref[...] + q[:, 2 * COLS :])


def rim(ret, slot, slot_cols, base, base_cols):
    return call(
        rim_kernel,
        edge_shapes(),
        (ret, slot, slot_cols, base[0:1], base[ROWS - 1 : ROWS], base_cols),
        [pltpu.VMEM((PAIRS * LEV, 256), BF16)],
    )


def unpack_kernel(ret_ref, slot_ref, base_ref, second_ref, r_ref):
    in_pairs(ret_ref, r_ref)
    for r in range(ROWS):
        q = picked(r_ref, slot_ref[r : r + 1, :])
        second_ref[r] = (base_ref[r] + 0.5 * q).astype(BF16)


def unpack(ret, slot, base):
    return call(
        unpack_kernel,
        jax.ShapeDtypeStruct((ROWS, LEV, COLS), BF16),
        (ret, slot, base),
        [pltpu.VMEM((PAIRS * LEV, 256), BF16)],
    )


def last_kernel(second_ref, above_ref, below_ref, left_ref, right_ref, out_ref, o_ref):
    row_of = lambda r: second_ref[r].astype(F32)
    for r, value in stencil_rows(row_of, above_ref, below_ref, left_ref, right_ref):
        o_ref[:, r, :] = value
    out_ref[...] = o_ref[...].astype(BF16)


def last_step(second, halo):
    return call(
        last_kernel,
        jax.ShapeDtypeStruct((LEV, ROWS, COLS), BF16),
        (second, *halo),
        [pltpu.VMEM((LEV, ROWS, COLS), F32)],
    )


def exchange(top, bottom, left, right):
    grp = lax.axis_size("grp")
    tile = lax.axis_size("tile")
    up = [(i, (i + 1) % grp) for i in range(grp)]
    along = [(i, (i + 1) % tile) for i in range(tile)]
    above = lax.ppermute(bottom, "grp", up)
    below = lax.ppermute(top, "grp", [(b, a) for a, b in up])
    west = lax.ppermute(right, "tile", along)
    east = lax.ppermute(left, "tile", [(b, a) for a, b in along])
    return above, below, west, east


def on_device(temp, humid, parent, kabs, planck, top_flux):
    send, slot = pack(temp, humid, parent)
    recv = lax.all_to_all(send, "tile", split_axis=0, concat_axis=0, tiled=True)
    base, base_cols, slot_cols = base_step(temp, humid, slot, exchange(*edges(temp)))
    recv, base, base_cols, slot_cols = lax.optimization_barrier((recv, base, base_cols, slot_cols))
    answer = owner_step(recv, kabs, planck, top_flux)
    ret = lax.all_to_all(answer, "tile", split_axis=0, concat_axis=0, tiled=True)
    halo = exchange(*rim(ret, slot, slot_cols, base, base_cols))
    second = unpack(ret, slot, base)
    return last_step(second, halo)


def solution(mesh):
    placed = (P(None, "grp", "tile"), P(None, "grp", "tile"), P("grp", "tile"), P(), P(), P())
    return jax.shard_map(
        on_device, mesh=mesh, in_specs=placed, out_specs=P(None, "grp", "tile"), check_vma=False
    )
```

```python
import jax
import jax.numpy as jnp
from jax import lax
from jax.experimental import pallas as pl
from jax.experimental.pallas import tpu as pltpu
from jax.sharding import PartitionSpec as P

F32 = jnp.float32
BF16 = jnp.bfloat16
LEV = 48
G = 112
ROWS = 16
COLS = 256
CELLS = ROWS * COLS
OWNED = 1024
TILES = 64
CAP = 128
PAIRS = TILES // 2
BLK_ROW = 96
ONE_ROW = 98
SEND = 104
WIDE = 112
GROUP = 8
GB = 4
LOG2E = 1.4426950408889634
VMEM = 32 * 1024 * 1024


def call(kernel, out_shape, operands, scratch=(), scalars=0, resident_in=True, resident_out=True):
    vmem = pl.BlockSpec(memory_space=pltpu.VMEM)
    smem = pl.BlockSpec(memory_space=pltpu.SMEM)
    many = isinstance(out_shape, tuple)
    arrays = len(operands) - scalars
    if resident_in:
        operands = [
            pltpu.with_memory_space_constraint(x, pltpu.VMEM) if i < arrays else x for i, x in enumerate(operands)
        ]
    if resident_out:
        place = lambda x: pltpu.VMEM(x.shape, x.dtype)
        out_shape = tuple(place(x) for x in out_shape) if many else place(out_shape)
    return pl.pallas_call(
        kernel,
        out_shape=out_shape,
        in_specs=[vmem] * arrays + [smem] * scalars,
        out_specs=(vmem,) * len(out_shape) if many else vmem,
        scratch_shapes=list(scratch),
        compiler_params=pltpu.CompilerParams(vmem_limit_bytes=VMEM),
    )(*operands)


def pack_kernel(temp_ref, humid_ref, parent_ref, send_ref, slot_ref,
                temp_in, humid_in, send_out, t_ref, h_ref, x_ref, b_ref, pair_ref, in_sem, out_sem):
    arriving = [
        pltpu.make_async_copy(temp_ref, temp_in, in_sem.at[0]),
        pltpu.make_async_copy(humid_ref, humid_in, in_sem.at[1]),
    ]
    for copy in arriving:
        copy.start()
    sub = lax.broadcasted_iota(jnp.int32, (COLS, COLS), 0)
    lane = lax.broadcasted_iota(jnp.int32, (COLS, COLS), 1)
    before = (sub < lane).astype(BF16)
    ones = jnp.ones((COLS, COLS), BF16)
    sub64 = lax.broadcasted_iota(jnp.int32, (TILES, COLS), 0)
    sub16 = lax.broadcasted_iota(jnp.int32, (16, COLS), 0)
    parent = parent_ref[...]
    owner = parent // OWNED
    local = parent % OWNED
    blk = (local // 256 + 1).astype(F32)
    low = (local % 256).astype(F32)
    hits = [jnp.where(owner[r : r + 1] == sub64, 1.0, 0.0).astype(F32) for r in range(ROWS)]
    stacked = jnp.concatenate([h.astype(BF16) for h in hits], axis=0)
    ranks = jnp.dot(stacked, before, preferred_element_type=F32)
    totals = jnp.dot(stacked, ones, preferred_element_type=F32)
    carry = jnp.zeros((TILES, COLS), F32)
    position = []
    for r in range(ROWS):
        span = slice(r * TILES, (r + 1) * TILES)
        position.append(jnp.sum(hits[r] * (ranks[span] + carry), axis=0, keepdims=True))
        carry = carry + totals[span]
    slot = owner * CAP + jnp.concatenate(position, axis=0).astype(jnp.int32)
    slot_ref[...] = slot
    pair = (slot // 256).astype(F32)
    within = (slot % 256).astype(F32).T.astype(BF16)
    for r in range(ROWS):
        cols = slice(r * COLS, (r + 1) * COLS)
        extra = jnp.where(
            sub16 == 0, blk[r : r + 1], jnp.where(sub16 == 1, low[r : r + 1], jnp.where(sub16 == 2, 1.0, 0.0))
        )
        x_ref[2 * LEV : WIDE, cols] = extra.astype(BF16)
        b_ref[cols, :] = hot_across(within[:, r : r + 1])
        pair_ref[:, cols] = jnp.broadcast_to(pair[r : r + 1], (16, COLS)).astype(BF16)

    for copy in arriving:
        copy.wait()
    t_ref[...] = temp_in[...].astype(F32)
    h_ref[...] = humid_in[...].astype(F32)
    for r in range(ROWS):
        cols = slice(r * COLS, (r + 1) * COLS)
        x_ref[0:LEV, cols] = t_ref[:, r, :].astype(BF16)
        x_ref[LEV : 2 * LEV, cols] = h_ref[:, r, :].astype(BF16)

    values = x_ref[...].reshape(WIDE // 16, 16, CELLS)
    leaving = []
    for step in range(PAIRS // GROUP):
        chosen = []
        for j in range(GROUP):
            mask = pair_ref[...] == jnp.asarray(step * GROUP + j, BF16)
            chosen.append(jnp.where(mask[None], values, jnp.zeros_like(values)).reshape(WIDE, CELLS))
        moved = jnp.dot(jnp.concatenate(chosen, axis=0), b_ref[...], preferred_element_type=F32)
        for j in range(GROUP):
            p = step * GROUP + j
            part = moved[j * WIDE : j * WIDE + SEND].astype(BF16)
            send_out[2 * p] = part[:, 0:CAP]
            send_out[2 * p + 1] = part[:, CAP : 2 * CAP]
        done = pl.ds(2 * step * GROUP, 2 * GROUP)
        copy = pltpu.make_async_copy(send_out.at[done], send_ref.at[done], out_sem.at[step])
        copy.start()
        leaving.append(copy)
    for copy in leaving:
        copy.wait()


def pack(temp, humid, parent):
    vmem = pl.BlockSpec(memory_space=pltpu.VMEM)
    hbm = pl.BlockSpec(memory_space=pltpu.HBM)
    field = (LEV, ROWS, COLS)
    return pl.pallas_call(
        pack_kernel,
        out_shape=(
            pltpu.HBM((TILES, SEND, CAP), BF16),
            pltpu.VMEM((ROWS, COLS), jnp.int32),
        ),
        in_specs=[hbm, hbm, vmem],
        out_specs=(hbm, vmem),
        scratch_shapes=[
            pltpu.VMEM(field, BF16),
            pltpu.VMEM(field, BF16),
            pltpu.VMEM((TILES, SEND, CAP), BF16),
            pltpu.VMEM(field, F32),
            pltpu.VMEM(field, F32),
            pltpu.VMEM((WIDE, CELLS), BF16),
            pltpu.VMEM((CELLS, COLS), BF16),
            pltpu.VMEM((16, CELLS), BF16),
            pltpu.SemaphoreType.DMA((2,)),
            pltpu.SemaphoreType.DMA((PAIRS // GROUP,)),
        ],
        compiler_params=pltpu.CompilerParams(vmem_limit_bytes=VMEM),
    )(
        pltpu.with_memory_space_constraint(temp, pltpu.HBM),
        pltpu.with_memory_space_constraint(humid, pltpu.HBM),
        parent,
    )


def hot_down(row):
    n = row.shape[1]
    index = lax.broadcasted_iota(jnp.int32, (256, n), 0).astype(F32).astype(BF16).reshape(16, 16, n)
    hit = index == jnp.broadcast_to(row, (16, n)).astype(BF16)[None]
    return jnp.where(hit, jnp.ones_like(index), jnp.zeros_like(index)).reshape(256, n)


def hot_across(column):
    n = column.shape[0]
    index = lax.broadcasted_iota(jnp.int32, (n, 256), 1).astype(F32).astype(BF16)
    hit = index == jnp.broadcast_to(column, (n, 256))
    return jnp.where(hit, jnp.ones_like(index), jnp.zeros_like(index))


def owner_kernel(recv_ref, kabs_ref, planck_ref, top_ref, out_ref,
                 b_ref, absorb_ref, emit_ref, step_ref, hmean_ref, net_ref, trans_ref, sum_ref, q_ref):
    lows = jnp.concatenate([recv_ref[s, BLK_ROW:SEND, :].astype(F32)[1:2] for s in range(TILES)], axis=0)
    low_cols = lows.T.astype(BF16)

    for first in range(0, TILES, 4):
        lhs = []
        rhs = []
        for s in range(first, first + 4):
            got = recv_ref[s]
            blk = jnp.broadcast_to(got[BLK_ROW:SEND].astype(F32)[0:1], (SEND, CAP)).astype(BF16)
            half = slice((s % 2) * CAP, (s % 2 + 1) * CAP)
            b_ref[s // 2, :, half] = hot_down(lows[s : s + 1])
            rhs.append(hot_across(low_cols[:, s : s + 1]))
            zero = jnp.zeros_like(got)
            lhs.append(
                jnp.concatenate([jnp.where(blk == jnp.asarray(b + 1, BF16), got, zero) for b in range(4)], axis=0)
            )
        part = jnp.dot(
            jnp.concatenate(lhs, axis=1), jnp.concatenate(rhs, axis=0), preferred_element_type=F32
        )
        if first == 0:
            sum_ref[...] = part
        else:
            sum_ref[...] += part

    counts = []
    for b in range(4):
        for h in range(2):
            lanes = slice(h * CAP, (h + 1) * CAP)
            row = b * SEND + ONE_ROW
            counts.append(sum_ref[row : row + 1, lanes])
            emit_ref[:, 2 * b + h, :] = sum_ref[b * SEND : b * SEND + LEV, lanes]
            hmean_ref[:, 2 * b + h, :] = sum_ref[b * SEND + LEV : b * SEND + 2 * LEV, lanes]
    inv = 1.0 / jnp.maximum(jnp.concatenate(counts, axis=0), 1.0)
    hc = hmean_ref[...] * inv[None]
    absorb_ref[...] = jnp.exp(0.5 * hc)
    emit = jnp.exp(0.25 * (emit_ref[...] * inv[None]))
    emit_ref[...] = emit
    step_ref[0 : LEV - 1] = emit[1:LEV] - emit[0 : LEV - 1]
    hmean_ref[...] = hc
    net_ref[...] = jnp.zeros_like(net_ref)
    emit_top = emit_ref[0]
    emit_low = emit_ref[LEV - 1]

    def one_block(block, top_net):
        first = block * GB
        tops = [top_ref[first + j] for j in range(GB)]
        planck = [planck_ref[first + j] for j in range(GB)]
        state = [tops[j] - emit_top * planck[j] for j in range(GB)]
        for k in range(LEV):
            absorb = absorb_ref[k]
            total = None
            for j in range(GB):
                t = jnp.exp2(absorb * kabs_ref[first + j, k])
                trans_ref[k, j] = t
                state[j] = t * state[j]
                total = state[j] if total is None else total + state[j]
            net_ref[k] += total
            if k < LEV - 1:
                step = step_ref[k]
                state = [state[j] - step * planck[j] for j in range(GB)]
        state = [
            0.3 * (state[j] + emit_low * planck[j]) - emit_low * planck[j] for j in range(GB)
        ]
        for k in range(LEV - 1, -1, -1):
            total = None
            for j in range(GB):
                state[j] = trans_ref[k, j] * state[j]
                total = state[j] if total is None else total + state[j]
            net_ref[k] -= total
            if k > 0:
                step = step_ref[k - 1]
                state = [state[j] + step * planck[j] for j in range(GB)]
        for j in range(GB):
            top_net = top_net + (tops[j] - (state[j] + emit_top * planck[j]))
        return top_net

    top_net = lax.fori_loop(0, G // GB, one_block, jnp.zeros((8, 128), F32))
    net = net_ref[...]
    prev = jnp.concatenate([top_net[None], net[:-1]], axis=0)
    heat = ((prev - net) * (LEV / G)).astype(BF16).astype(F32)
    hm = hmean_ref[...].astype(BF16).astype(F32)
    net_ref[...] = heat - 0.5 * hm
    for b in range(4):
        for h in range(2):
            q_ref[b * LEV : (b + 1) * LEV, h * CAP : (h + 1) * CAP] = net_ref[:, 2 * b + h, :].astype(BF16)

    for p in range(PAIRS):
        both = jnp.dot(q_ref[...], b_ref[p], preferred_element_type=F32)
        for h in range(2):
            lanes = slice(h * CAP, (h + 1) * CAP)
            blk = recv_ref[2 * p + h, BLK_ROW:SEND, :].astype(F32)[0:1]
            got = jnp.zeros((LEV, CAP), F32)
            for b in range(4):
                got = jnp.where(blk == float(b + 1), both[b * LEV : (b + 1) * LEV, lanes], got)
            out_ref[2 * p + h] = got.astype(BF16)


def owner_step(recv, kabs, planck, top_flux):
    column = pltpu.VMEM((LEV, 8, 128), F32)
    return call(
        owner_kernel,
        jax.ShapeDtypeStruct((TILES, LEV, CAP), BF16),
        (recv, kabs * (-LOG2E), planck, top_flux),
        [
            pltpu.VMEM((PAIRS, 256, 256), BF16),
            column,
            column,
            column,
            column,
            column,
            pltpu.VMEM((LEV, GB, 8, 128), F32),
            pltpu.VMEM((4 * SEND, 256), F32),
            pltpu.VMEM((4 * LEV, 256), BF16),
        ],
        scalars=3,
    )


def gather_columns(row_of):
    first = row_of(0)
    lane = lax.broadcasted_iota(jnp.int32, (first.shape[0], 128), 1)
    kept = jnp.zeros((first.shape[0], 128), first.dtype)
    for r in range(ROWS):
        row = row_of(r)
        kept = jnp.where(lane == r, row[:, 0:1], kept)
        kept = jnp.where(lane == ROWS + r, row[:, COLS - 1 : COLS], kept)
    return kept


def split_columns(columns):
    return columns.astype(BF16), pltpu.roll(columns, 128 - ROWS, axis=1).astype(BF16)


def edge_shapes():
    row = jax.ShapeDtypeStruct((LEV, COLS), BF16)
    column = jax.ShapeDtypeStruct((LEV, 128), BF16)
    return row, row, column, column


def edges_kernel(temp_ref, top_ref, bottom_ref, left_ref, right_ref, t_ref):
    t_ref[...] = temp_ref[...].astype(F32)
    top_ref[...] = t_ref[:, 0, :].astype(BF16)
    bottom_ref[...] = t_ref[:, ROWS - 1, :].astype(BF16)
    left_ref[...], right_ref[...] = split_columns(gather_columns(lambda r: t_ref[:, r, :]))


def edges(temp):
    return call(
        edges_kernel, edge_shapes(), (temp,), [pltpu.VMEM((LEV, ROWS, COLS), F32)], resident_in=False
    )


def stencil_row(value, above, below, left, right):
    lane = lax.broadcasted_iota(jnp.int32, value.shape, 1)
    west = jnp.where(lane == 0, left, pltpu.roll(value, 1, axis=1))
    east = jnp.where(lane == COLS - 1, right, pltpu.roll(value, COLS - 1, axis=1))
    return value + 0.2 * (above + below + west + east - 4.0 * value)


def stencil_rows(row_of, above_ref, below_ref, left_ref, right_ref):
    left = left_ref[...].astype(F32)
    right = right_ref[...].astype(F32)
    above = above_ref[...].astype(F32)
    value = row_of(0)
    for r in range(ROWS):
        below = row_of(r + 1) if r < ROWS - 1 else below_ref[...].astype(F32)
        yield r, stencil_row(value, above, below, left[:, r : r + 1], right[:, r : r + 1])
        above, value = value, below


def base_kernel(temp_ref, humid_ref, slot_ref, above_ref, below_ref, left_ref, right_ref,
                base_ref, base_cols_ref, slot_cols_ref, t_ref, h_ref):
    t_ref[...] = temp_ref[...].astype(F32)
    h_ref[...] = humid_ref[...].astype(F32)
    for r, first in stencil_rows(lambda r: t_ref[:, r, :], above_ref, below_ref, left_ref, right_ref):
        base_ref[r] = first.astype(BF16).astype(F32) + 0.25 * h_ref[:, r, :]
    base_cols_ref[...] = gather_columns(lambda r: base_ref[r])
    slot = slot_ref[...]
    slots = gather_columns(lambda r: slot[r : r + 1])
    slot_cols_ref[...] = jnp.broadcast_to(slots, (8, 128))


def base_step(temp, humid, slot, halo):
    return call(
        base_kernel,
        (
            jax.ShapeDtypeStruct((ROWS, LEV, COLS), F32),
            jax.ShapeDtypeStruct((LEV, 128), F32),
            jax.ShapeDtypeStruct((8, 128), jnp.int32),
        ),
        (temp, humid, slot, *halo),
        [pltpu.VMEM((LEV, ROWS, COLS), F32), pltpu.VMEM((LEV, ROWS, COLS), F32)],
    )


def in_pairs(ret_ref, r_ref):
    for p in range(PAIRS):
        for h in range(2):
            r_ref[p * LEV : (p + 1) * LEV, h * CAP : (h + 1) * CAP] = ret_ref[2 * p + h]


def picked(r_ref, slot):
    count = slot.shape[1]
    pair = slot // 256
    moved = jnp.dot(r_ref[...], hot_down((slot % 256).astype(F32)), preferred_element_type=F32)
    q = jnp.zeros((LEV, count), F32)
    for p in range(PAIRS):
        q = jnp.where(pair == p, moved[p * LEV : (p + 1) * LEV], q)
    return q


def rim_kernel(ret_ref, slot_ref, slot_cols_ref, base_ref, base_cols_ref,
               top_ref, bottom_ref, left_ref, right_ref, r_ref):
    in_pairs(ret_ref, r_ref)
    slot = jnp.concatenate(
        [slot_ref[0:1, :], slot_ref[ROWS - 1 : ROWS, :], slot_cols_ref[0:1, :]], axis=1
    )
    q = 0.5 * picked(r_ref, slot)
    top_ref[...] = (base_ref[0] + q[:, 0:COLS]).astype(BF16)
    bottom_ref[...] = (base_ref[ROWS - 1] + q[:, COLS : 2 * COLS]).astype(BF16)
    left_ref[...], right_ref[...] = split_columns(base_cols_ref[...] + q[:, 2 * COLS :])


def rim(ret, slot, slot_cols, base, base_cols):
    return call(
        rim_kernel,
        edge_shapes(),
        (ret, slot, slot_cols, base, base_cols),
        [pltpu.VMEM((PAIRS * LEV, 256), BF16)],
    )


def unpack_kernel(ret_ref, slot_ref, base_ref, second_ref, r_ref):
    in_pairs(ret_ref, r_ref)
    for r in range(ROWS):
        q = picked(r_ref, slot_ref[r : r + 1, :])
        second_ref[r] = (base_ref[r] + 0.5 * q).astype(BF16)


def unpack(ret, slot, base):
    return call(
        unpack_kernel,
        jax.ShapeDtypeStruct((ROWS, LEV, COLS), BF16),
        (ret, slot, base),
        [pltpu.VMEM((PAIRS * LEV, 256), BF16)],
    )


def last_kernel(second_ref, above_ref, below_ref, left_ref, right_ref, out_ref, o_ref):
    row_of = lambda r: second_ref[r].astype(F32)
    for r, value in stencil_rows(row_of, above_ref, below_ref, left_ref, right_ref):
        o_ref[:, r, :] = value
    out_ref[...] = o_ref[...].astype(BF16)


def last_step(second, halo):
    return call(
        last_kernel,
        jax.ShapeDtypeStruct((LEV, ROWS, COLS), BF16),
        (second, *halo),
        [pltpu.VMEM((LEV, ROWS, COLS), F32)],
        resident_out=False,
    )


def exchange(top, bottom, left, right):
    grp = lax.axis_size("grp")
    tile = lax.axis_size("tile")
    up = [(i, (i + 1) % grp) for i in range(grp)]
    along = [(i, (i + 1) % tile) for i in range(tile)]
    above = lax.ppermute(bottom, "grp", up)
    below = lax.ppermute(top, "grp", [(b, a) for a, b in up])
    west = lax.ppermute(right, "tile", along)
    east = lax.ppermute(left, "tile", [(b, a) for a, b in along])
    return above, below, west, east


def on_device(temp, humid, parent, kabs, planck, top_flux):
    send, slot = pack(temp, humid, parent)
    recv = lax.all_to_all(send, "tile", split_axis=0, concat_axis=0, tiled=True)
    recv, halo = lax.optimization_barrier((recv, exchange(*edges(temp))))
    answer = owner_step(recv, kabs, planck, top_flux)
    answer, halo = lax.optimization_barrier((answer, halo))
    ret = lax.all_to_all(answer, "tile", split_axis=0, concat_axis=0, tiled=True)
    base, base_cols, slot_cols = base_step(temp, humid, slot, halo)
    halo = exchange(*rim(ret, slot, slot_cols, base, base_cols))
    second = unpack(ret, slot, base)
    return last_step(second, halo)


def solution(mesh):
    placed = (P(None, "grp", "tile"), P(None, "grp", "tile"), P("grp", "tile"), P(), P(), P())
    return jax.shard_map(
        on_device, mesh=mesh, in_specs=placed, out_specs=P(None, "grp", "tile"), check_vma=False
    )
```

```python
import jax
import jax.numpy as jnp
from jax import lax
from jax.experimental import pallas as pl
from jax.experimental.pallas import tpu as pltpu
from jax.sharding import PartitionSpec as P

F32 = jnp.float32
BF16 = jnp.bfloat16
LEV = 48
G = 112
ROWS = 16
COLS = 256
CELLS = ROWS * COLS
OWNED = 1024
TILES = 64
CAP = 128
PAIRS = TILES // 2
BLK_ROW = 96
ONE_ROW = 98
SEND = 104
VALUES = 96
GROUP = 8
GB = 7
LOG2E = 1.4426950408889634
VMEM = 32 * 1024 * 1024


def call(kernel, out_shape, operands, scratch=(), scalars=0, resident_in=True, out_space=pltpu.VMEM):
    vmem = pl.BlockSpec(memory_space=pltpu.VMEM)
    smem = pl.BlockSpec(memory_space=pltpu.SMEM)
    many = isinstance(out_shape, tuple)
    arrays = len(operands) - scalars
    if resident_in:
        operands = [
            pltpu.with_memory_space_constraint(x, pltpu.VMEM) if i < arrays else x for i, x in enumerate(operands)
        ]
    if out_space is not None:
        place = lambda x: out_space(x.shape, x.dtype)
        out_shape = tuple(place(x) for x in out_shape) if many else place(out_shape)
    out = pl.BlockSpec(memory_space=pltpu.HBM if out_space is pltpu.HBM else pltpu.VMEM)
    return pl.pallas_call(
        kernel,
        out_shape=out_shape,
        in_specs=[vmem] * arrays + [smem] * scalars,
        out_specs=(out,) * len(out_shape) if many else out,
        scratch_shapes=list(scratch),
        compiler_params=pltpu.CompilerParams(vmem_limit_bytes=VMEM),
    )(*operands)


def pack_kernel(temp_ref, humid_ref, parent_ref, send_ref, slot_ref,
                temp_in, humid_in, send_out, t_ref, h_ref, x_ref, l_ref, b_ref, pair_ref, in_sem, out_sem):
    arriving = [
        pltpu.make_async_copy(temp_ref, temp_in, in_sem.at[0]),
        pltpu.make_async_copy(humid_ref, humid_in, in_sem.at[1]),
    ]
    for copy in arriving:
        copy.start()
    sub = lax.broadcasted_iota(jnp.int32, (COLS, COLS), 0)
    lane = lax.broadcasted_iota(jnp.int32, (COLS, COLS), 1)
    before = (sub < lane).astype(BF16)
    ones = jnp.ones((COLS, COLS), BF16)
    sub64 = lax.broadcasted_iota(jnp.int32, (TILES, COLS), 0)
    sub8 = lax.broadcasted_iota(jnp.int32, (8, COLS), 0)
    parent = parent_ref[...]
    owner = parent // OWNED
    local = parent % OWNED
    blk = (local // 256 + 1).astype(F32)
    low = (local % 256).astype(F32)
    hits = [jnp.where(owner[r : r + 1] == sub64, 1.0, 0.0).astype(F32) for r in range(ROWS)]
    stacked = jnp.concatenate([h.astype(BF16) for h in hits], axis=0)
    ranks = jnp.dot(stacked, before, preferred_element_type=F32)
    totals = jnp.dot(stacked, ones, preferred_element_type=F32)
    carry = jnp.zeros((TILES, COLS), F32)
    position = []
    for r in range(ROWS):
        span = slice(r * TILES, (r + 1) * TILES)
        position.append(jnp.sum(hits[r] * (ranks[span] + carry), axis=0, keepdims=True))
        carry = carry + totals[span]
    slot = owner * CAP + jnp.concatenate(position, axis=0).astype(jnp.int32)
    slot_ref[...] = slot
    pair = (slot // 256).astype(F32)
    within = (slot % 256).astype(F32).T.astype(BF16)
    for r in range(ROWS):
        cols = slice(r * COLS, (r + 1) * COLS)
        l_ref[:, cols] = jnp.where(
            sub8 == 0, blk[r : r + 1], jnp.where(sub8 == 1, low[r : r + 1], jnp.where(sub8 == 2, 1.0, 0.0))
        )
        b_ref[cols, :] = hot_across(within[:, r : r + 1])
        pair_ref[:, cols] = jnp.broadcast_to(pair[r : r + 1], (16, COLS)).astype(BF16)

    for copy in arriving:
        copy.wait()
    t_ref[...] = temp_in[...].astype(F32)
    h_ref[...] = humid_in[...].astype(F32)
    for r in range(ROWS):
        cols = slice(r * COLS, (r + 1) * COLS)
        x_ref[0:LEV, cols] = t_ref[:, r, :].astype(BF16)
        x_ref[LEV : 2 * LEV, cols] = h_ref[:, r, :].astype(BF16)

    values = x_ref[...].reshape(VALUES // 16, 16, CELLS)
    labels = l_ref[...]
    leaving = []
    for step in range(PAIRS // GROUP):
        chosen = []
        extra = []
        for j in range(GROUP):
            p = step * GROUP + j
            mask = pair_ref[...] == jnp.asarray(p, BF16)
            chosen.append(jnp.where(mask[None], values, jnp.zeros_like(values)).reshape(VALUES, CELLS))
            extra.append(jnp.where(pair_ref[0:8, :].astype(F32) == float(p), labels, 0.0))
        chosen.append(jnp.concatenate(extra, axis=0).astype(BF16))
        moved = jnp.dot(jnp.concatenate(chosen, axis=0), b_ref[...], preferred_element_type=F32).astype(BF16)
        for j in range(GROUP):
            p = step * GROUP + j
            part = moved[j * VALUES : (j + 1) * VALUES]
            label = moved[GROUP * VALUES + 8 * j : GROUP * VALUES + 8 * (j + 1)]
            for h in range(2):
                send_out[2 * p + h, 0:VALUES, :] = part[:, h * CAP : (h + 1) * CAP]
                send_out[2 * p + h, VALUES:SEND, :] = label[:, h * CAP : (h + 1) * CAP]
        done = pl.ds(2 * step * GROUP, 2 * GROUP)
        copy = pltpu.make_async_copy(send_out.at[done], send_ref.at[done], out_sem.at[step])
        copy.start()
        leaving.append(copy)
    for copy in leaving:
        copy.wait()


def pack(temp, humid, parent):
    vmem = pl.BlockSpec(memory_space=pltpu.VMEM)
    hbm = pl.BlockSpec(memory_space=pltpu.HBM)
    field = (LEV, ROWS, COLS)
    return pl.pallas_call(
        pack_kernel,
        out_shape=(
            pltpu.HBM((TILES, SEND, CAP), BF16),
            pltpu.VMEM((ROWS, COLS), jnp.int32),
        ),
        in_specs=[hbm, hbm, vmem],
        out_specs=(hbm, vmem),
        scratch_shapes=[
            pltpu.VMEM(field, BF16),
            pltpu.VMEM(field, BF16),
            pltpu.VMEM((TILES, SEND, CAP), BF16),
            pltpu.VMEM(field, F32),
            pltpu.VMEM(field, F32),
            pltpu.VMEM((VALUES, CELLS), BF16),
            pltpu.VMEM((8, CELLS), F32),
            pltpu.VMEM((CELLS, COLS), BF16),
            pltpu.VMEM((16, CELLS), BF16),
            pltpu.SemaphoreType.DMA((2,)),
            pltpu.SemaphoreType.DMA((PAIRS // GROUP,)),
        ],
        compiler_params=pltpu.CompilerParams(vmem_limit_bytes=VMEM),
    )(
        pltpu.with_memory_space_constraint(temp, pltpu.HBM),
        pltpu.with_memory_space_constraint(humid, pltpu.HBM),
        parent,
    )


def hot_down(row):
    n = row.shape[1]
    index = lax.broadcasted_iota(jnp.int32, (256, n), 0).astype(F32).astype(BF16).reshape(16, 16, n)
    hit = index == jnp.broadcast_to(row, (16, n)).astype(BF16)[None]
    return jnp.where(hit, jnp.ones_like(index), jnp.zeros_like(index)).reshape(256, n)


def hot_across(column):
    n = column.shape[0]
    index = lax.broadcasted_iota(jnp.int32, (n, 256), 1).astype(F32).astype(BF16)
    hit = index == jnp.broadcast_to(column, (n, 256))
    return jnp.where(hit, jnp.ones_like(index), jnp.zeros_like(index))


def owner_kernel(recv_ref, kabs_ref, planck_ref, top_ref, out_ref,
                 b_ref, absorb_ref, emit_ref, step_ref, hmean_ref, net_ref, trans_ref, rise_ref, sum_ref, q_ref,
                 answer_ref, out_sem):
    lows = jnp.concatenate([recv_ref[s, BLK_ROW:SEND, :].astype(F32)[1:2] for s in range(TILES)], axis=0)
    low_cols = lows.T.astype(BF16)

    for first in range(0, TILES, 4):
        lhs = []
        rhs = []
        for s in range(first, first + 4):
            got = recv_ref[s]
            blk = jnp.broadcast_to(got[BLK_ROW:SEND].astype(F32)[0:1], (SEND, CAP)).astype(BF16)
            half = slice((s % 2) * CAP, (s % 2 + 1) * CAP)
            b_ref[s // 2, :, half] = hot_down(lows[s : s + 1])
            rhs.append(hot_across(low_cols[:, s : s + 1]))
            zero = jnp.zeros_like(got)
            lhs.append(
                jnp.concatenate([jnp.where(blk == jnp.asarray(b + 1, BF16), got, zero) for b in range(4)], axis=0)
            )
        part = jnp.dot(
            jnp.concatenate(lhs, axis=1), jnp.concatenate(rhs, axis=0), preferred_element_type=F32
        )
        if first == 0:
            sum_ref[...] = part
        else:
            sum_ref[...] += part

    counts = []
    for b in range(4):
        for h in range(2):
            lanes = slice(h * CAP, (h + 1) * CAP)
            row = b * SEND + ONE_ROW
            counts.append(sum_ref[row : row + 1, lanes])
            emit_ref[:, 2 * b + h, :] = sum_ref[b * SEND : b * SEND + LEV, lanes]
            hmean_ref[:, 2 * b + h, :] = sum_ref[b * SEND + LEV : b * SEND + 2 * LEV, lanes]
    inv = 1.0 / jnp.maximum(jnp.concatenate(counts, axis=0), 1.0)
    hc = hmean_ref[...] * inv[None]
    absorb_ref[...] = jnp.exp(0.5 * hc)
    emit = jnp.exp(0.25 * (emit_ref[...] * inv[None]))
    emit_ref[...] = emit
    step_ref[0 : LEV - 1] = emit[1:LEV] - emit[0 : LEV - 1]
    hmean_ref[...] = hc
    net_ref[...] = jnp.zeros_like(net_ref)
    emit_top = emit_ref[0]
    emit_low = emit_ref[LEV - 1]

    def one_block(block, top_net):
        first = block * GB
        tops = [top_ref[first + j] for j in range(GB)]
        planck = [planck_ref[first + j] for j in range(GB)]
        state = [tops[j] - emit_top * planck[j] for j in range(GB)]
        for k in range(LEV):
            absorb = absorb_ref[k]
            total = None
            for j in range(GB):
                t = jnp.exp2(absorb * kabs_ref[first + j, k])
                trans_ref[k, j] = t
                state[j] = t * state[j]
                total = state[j] if total is None else total + state[j]
            net_ref[k] += total
            if k < LEV - 1:
                step = step_ref[k]
                for j in range(GB):
                    rise = step * planck[j]
                    rise_ref[k, j] = rise
                    state[j] = state[j] - rise
        state = [
            0.3 * (state[j] + emit_low * planck[j]) - emit_low * planck[j] for j in range(GB)
        ]
        for k in range(LEV - 1, -1, -1):
            total = None
            for j in range(GB):
                state[j] = trans_ref[k, j] * state[j]
                total = state[j] if total is None else total + state[j]
            net_ref[k] -= total
            if k > 0:
                state = [state[j] + rise_ref[k - 1, j] for j in range(GB)]
        for j in range(GB):
            top_net = top_net + (tops[j] - (state[j] + emit_top * planck[j]))
        return top_net

    top_net = lax.fori_loop(0, G // GB, one_block, jnp.zeros((8, 128), F32), unroll=2)
    net = net_ref[...]
    prev = jnp.concatenate([top_net[None], net[:-1]], axis=0)
    heat = ((prev - net) * (LEV / G)).astype(BF16).astype(F32)
    hm = hmean_ref[...].astype(BF16).astype(F32)
    net_ref[...] = heat - 0.5 * hm
    for b in range(4):
        for h in range(2):
            q_ref[b * LEV : (b + 1) * LEV, h * CAP : (h + 1) * CAP] = net_ref[:, 2 * b + h, :].astype(BF16)

    leaving = []
    for p in range(PAIRS):
        both = jnp.dot(q_ref[...], b_ref[p], preferred_element_type=F32)
        for h in range(2):
            lanes = slice(h * CAP, (h + 1) * CAP)
            blk = recv_ref[2 * p + h, BLK_ROW:SEND, :].astype(F32)[0:1]
            got = jnp.zeros((LEV, CAP), F32)
            for b in range(4):
                got = jnp.where(blk == float(b + 1), both[b * LEV : (b + 1) * LEV, lanes], got)
            answer_ref[2 * p + h] = got.astype(BF16)
        if p % (PAIRS // 4) == PAIRS // 4 - 1:
            step = p // (PAIRS // 4)
            done = pl.ds(step * (TILES // 4), TILES // 4)
            copy = pltpu.make_async_copy(answer_ref.at[done], out_ref.at[done], out_sem.at[step])
            copy.start()
            leaving.append(copy)
    for copy in leaving:
        copy.wait()


def owner_step(recv, kabs, planck, top_flux):
    column = pltpu.VMEM((LEV, 8, 128), F32)
    return call(
        owner_kernel,
        jax.ShapeDtypeStruct((TILES, LEV, CAP), BF16),
        (recv, kabs * (-LOG2E), planck, top_flux),
        [
            pltpu.VMEM((PAIRS, 256, 256), BF16),
            column,
            column,
            column,
            column,
            column,
            pltpu.VMEM((LEV, GB, 8, 128), F32),
            pltpu.VMEM((LEV, GB, 8, 128), F32),
            pltpu.VMEM((4 * SEND, 256), F32),
            pltpu.VMEM((4 * LEV, 256), BF16),
            pltpu.VMEM((TILES, LEV, CAP), BF16),
            pltpu.SemaphoreType.DMA((4,)),
        ],
        scalars=3,
        out_space=pltpu.HBM,
    )


def gather_columns(row_of):
    first = row_of(0)
    lane = lax.broadcasted_iota(jnp.int32, (first.shape[0], 128), 1)
    kept = jnp.zeros((first.shape[0], 128), first.dtype)
    for r in range(ROWS):
        row = row_of(r)
        kept = jnp.where(lane == r, row[:, 0:1], kept)
        kept = jnp.where(lane == ROWS + r, row[:, COLS - 1 : COLS], kept)
    return kept


def split_columns(columns):
    return columns.astype(BF16), pltpu.roll(columns, 128 - ROWS, axis=1).astype(BF16)


def edge_shapes():
    row = jax.ShapeDtypeStruct((LEV, COLS), BF16)
    column = jax.ShapeDtypeStruct((LEV, 128), BF16)
    return row, row, column, column


def edges_kernel(temp_ref, top_ref, bottom_ref, left_ref, right_ref, t_ref):
    t_ref[...] = temp_ref[...].astype(F32)
    top_ref[...] = t_ref[:, 0, :].astype(BF16)
    bottom_ref[...] = t_ref[:, ROWS - 1, :].astype(BF16)
    left_ref[...], right_ref[...] = split_columns(gather_columns(lambda r: t_ref[:, r, :]))


def edges(temp):
    return call(
        edges_kernel, edge_shapes(), (temp,), [pltpu.VMEM((LEV, ROWS, COLS), F32)], resident_in=False
    )


def stencil_row(value, above, below, left, right):
    lane = lax.broadcasted_iota(jnp.int32, value.shape, 1)
    west = jnp.where(lane == 0, left, pltpu.roll(value, 1, axis=1))
    east = jnp.where(lane == COLS - 1, right, pltpu.roll(value, COLS - 1, axis=1))
    return value + 0.2 * (above + below + west + east - 4.0 * value)


def stencil_rows(row_of, above_ref, below_ref, left_ref, right_ref):
    left = left_ref[...].astype(F32)
    right = right_ref[...].astype(F32)
    above = above_ref[...].astype(F32)
    value = row_of(0)
    for r in range(ROWS):
        below = row_of(r + 1) if r < ROWS - 1 else below_ref[...].astype(F32)
        yield r, stencil_row(value, above, below, left[:, r : r + 1], right[:, r : r + 1])
        above, value = value, below


def base_kernel(temp_ref, humid_ref, slot_ref, above_ref, below_ref, left_ref, right_ref,
                base_ref, base_cols_ref, slot_cols_ref, t_ref, h_ref):
    t_ref[...] = temp_ref[...].astype(F32)
    h_ref[...] = humid_ref[...].astype(F32)
    for r, first in stencil_rows(lambda r: t_ref[:, r, :], above_ref, below_ref, left_ref, right_ref):
        base_ref[r] = first.astype(BF16).astype(F32) + 0.25 * h_ref[:, r, :]
    base_cols_ref[...] = gather_columns(lambda r: base_ref[r])
    slot = slot_ref[...]
    slots = gather_columns(lambda r: slot[r : r + 1])
    slot_cols_ref[...] = jnp.broadcast_to(slots, (8, 128))


def base_step(temp, humid, slot, halo):
    return call(
        base_kernel,
        (
            jax.ShapeDtypeStruct((ROWS, LEV, COLS), F32),
            jax.ShapeDtypeStruct((LEV, 128), F32),
            jax.ShapeDtypeStruct((8, 128), jnp.int32),
        ),
        (temp, humid, slot, *halo),
        [pltpu.VMEM((LEV, ROWS, COLS), F32), pltpu.VMEM((LEV, ROWS, COLS), F32)],
    )


def in_pairs(ret_ref, r_ref):
    for p in range(PAIRS):
        for h in range(2):
            r_ref[p * LEV : (p + 1) * LEV, h * CAP : (h + 1) * CAP] = ret_ref[2 * p + h]


def picked(r_ref, slot):
    count = slot.shape[1]
    pair = slot // 256
    moved = jnp.dot(r_ref[...], hot_down((slot % 256).astype(F32)), preferred_element_type=F32)
    q = jnp.zeros((LEV, count), F32)
    for p in range(PAIRS):
        q = jnp.where(pair == p, moved[p * LEV : (p + 1) * LEV], q)
    return q


def rim_kernel(ret_ref, slot_ref, slot_cols_ref, base_ref, base_cols_ref,
               top_ref, bottom_ref, left_ref, right_ref, r_ref):
    in_pairs(ret_ref, r_ref)
    slot = jnp.concatenate(
        [slot_ref[0:1, :], slot_ref[ROWS - 1 : ROWS, :], slot_cols_ref[0:1, :]], axis=1
    )
    q = 0.5 * picked(r_ref, slot)
    top_ref[...] = (base_ref[0] + q[:, 0:COLS]).astype(BF16)
    bottom_ref[...] = (base_ref[ROWS - 1] + q[:, COLS : 2 * COLS]).astype(BF16)
    left_ref[...], right_ref[...] = split_columns(base_cols_ref[...] + q[:, 2 * COLS :])


def rim(ret, slot, slot_cols, base, base_cols):
    return call(
        rim_kernel,
        edge_shapes(),
        (ret, slot, slot_cols, base, base_cols),
        [pltpu.VMEM((PAIRS * LEV, 256), BF16)],
    )


def unpack_kernel(ret_ref, slot_ref, base_ref, top_ref, bottom_ref, second_ref, r_ref):
    in_pairs(ret_ref, r_ref)
    second_ref[0] = top_ref[...]
    second_ref[ROWS - 1] = bottom_ref[...]
    for r in range(1, ROWS - 1):
        q = picked(r_ref, slot_ref[r : r + 1, :])
        second_ref[r] = (base_ref[r] + 0.5 * q).astype(BF16)


def unpack(ret, slot, base, top, bottom):
    return call(
        unpack_kernel,
        jax.ShapeDtypeStruct((ROWS, LEV, COLS), BF16),
        (ret, slot, base, top, bottom),
        [pltpu.VMEM((PAIRS * LEV, 256), BF16)],
    )


def last_kernel(second_ref, above_ref, below_ref, left_ref, right_ref, out_ref, o_ref):
    row_of = lambda r: second_ref[r].astype(F32)
    for r, value in stencil_rows(row_of, above_ref, below_ref, left_ref, right_ref):
        o_ref[:, r, :] = value
    out_ref[...] = o_ref[...].astype(BF16)


def last_step(second, halo):
    return call(
        last_kernel,
        jax.ShapeDtypeStruct((LEV, ROWS, COLS), BF16),
        (second, *halo),
        [pltpu.VMEM((LEV, ROWS, COLS), F32)],
        out_space=None,
    )


def exchange(top, bottom, left, right):
    grp = lax.axis_size("grp")
    tile = lax.axis_size("tile")
    up = [(i, (i + 1) % grp) for i in range(grp)]
    along = [(i, (i + 1) % tile) for i in range(tile)]
    above = lax.ppermute(bottom, "grp", up)
    below = lax.ppermute(top, "grp", [(b, a) for a, b in up])
    west = lax.ppermute(right, "tile", along)
    east = lax.ppermute(left, "tile", [(b, a) for a, b in along])
    return above, below, west, east


def on_device(temp, humid, parent, kabs, planck, top_flux):
    send, slot = pack(temp, humid, parent)
    recv = lax.all_to_all(send, "tile", split_axis=0, concat_axis=0, tiled=True)
    recv, halo = lax.optimization_barrier((recv, exchange(*edges(temp))))
    answer = owner_step(recv, kabs, planck, top_flux)
    answer, halo = lax.optimization_barrier((answer, halo))
    ret = lax.all_to_all(answer, "tile", split_axis=0, concat_axis=0, tiled=True)
    base, base_cols, slot_cols = base_step(temp, humid, slot, halo)
    top, bottom, left, right = rim(ret, slot, slot_cols, base, base_cols)
    halo = exchange(top, bottom, left, right)
    second = unpack(ret, slot, base, top, bottom)
    return last_step(second, halo)


def solution(mesh):
    placed = (P(None, "grp", "tile"), P(None, "grp", "tile"), P("grp", "tile"), P(), P(), P())
    return jax.shard_map(
        on_device, mesh=mesh, in_specs=placed, out_specs=P(None, "grp", "tile"), check_vma=False
    )
```

```python
import jax
import jax.numpy as jnp
from jax import lax
from jax.experimental import pallas as pl
from jax.experimental.pallas import tpu as pltpu
from jax.sharding import PartitionSpec as P

F32 = jnp.float32
BF16 = jnp.bfloat16
LEV = 48
G = 112
ROWS = 16
COLS = 256
CELLS = ROWS * COLS
OWNED = 1024
TILES = 64
CAP = 128
PAIRS = TILES // 2
BLK_ROW = 96
ONE_ROW = 98
SEND = 104
VALUES = 96
GROUP = 8
GB = 7
LOG2E = 1.4426950408889634
VMEM = 32 * 1024 * 1024


def call(kernel, out_shape, operands, scratch=(), scalars=0, resident_in=True, out_space=pltpu.VMEM):
    vmem = pl.BlockSpec(memory_space=pltpu.VMEM)
    smem = pl.BlockSpec(memory_space=pltpu.SMEM)
    many = isinstance(out_shape, tuple)
    arrays = len(operands) - scalars
    if resident_in:
        operands = [
            pltpu.with_memory_space_constraint(x, pltpu.VMEM) if i < arrays else x for i, x in enumerate(operands)
        ]
    if out_space is not None:
        place = lambda x: out_space(x.shape, x.dtype)
        out_shape = tuple(place(x) for x in out_shape) if many else place(out_shape)
    out = pl.BlockSpec(memory_space=pltpu.HBM if out_space is pltpu.HBM else pltpu.VMEM)
    return pl.pallas_call(
        kernel,
        out_shape=out_shape,
        in_specs=[vmem] * arrays + [smem] * scalars,
        out_specs=(out,) * len(out_shape) if many else out,
        scratch_shapes=list(scratch),
        compiler_params=pltpu.CompilerParams(vmem_limit_bytes=VMEM),
    )(*operands)


def pack_kernel(temp_ref, humid_ref, parent_ref, send_ref, slot_ref,
                temp_in, humid_in, parent_in, send_out, t_ref, h_ref, x_ref, l_ref, b_ref, pair_ref, in_sem, out_sem):
    arriving = [
        pltpu.make_async_copy(temp_ref, temp_in, in_sem.at[0]),
        pltpu.make_async_copy(humid_ref, humid_in, in_sem.at[1]),
    ]
    named = pltpu.make_async_copy(parent_ref, parent_in, in_sem.at[2])
    named.start()
    for copy in arriving:
        copy.start()
    sub = lax.broadcasted_iota(jnp.int32, (COLS, COLS), 0)
    lane = lax.broadcasted_iota(jnp.int32, (COLS, COLS), 1)
    before = (sub < lane).astype(BF16)
    ones = jnp.ones((COLS, COLS), BF16)
    sub64 = lax.broadcasted_iota(jnp.int32, (TILES, COLS), 0)
    sub8 = lax.broadcasted_iota(jnp.int32, (8, COLS), 0)
    named.wait()
    parent = parent_in[...]
    owner = parent // OWNED
    local = parent % OWNED
    blk = (local // 256 + 1).astype(F32)
    low = (local % 256).astype(F32)
    hits = [jnp.where(owner[r : r + 1] == sub64, 1.0, 0.0).astype(F32) for r in range(ROWS)]
    stacked = jnp.concatenate([h.astype(BF16) for h in hits], axis=0)
    ranks = jnp.dot(stacked, before, preferred_element_type=F32)
    totals = jnp.dot(stacked, ones, preferred_element_type=F32)
    carry = jnp.zeros((TILES, COLS), F32)
    position = []
    for r in range(ROWS):
        span = slice(r * TILES, (r + 1) * TILES)
        position.append(jnp.sum(hits[r] * (ranks[span] + carry), axis=0, keepdims=True))
        carry = carry + totals[span]
    slot = owner * CAP + jnp.concatenate(position, axis=0).astype(jnp.int32)
    slot_ref[...] = slot
    pair = (slot // 256).astype(F32)
    within = (slot % 256).astype(F32).T.astype(BF16)
    for r in range(ROWS):
        cols = slice(r * COLS, (r + 1) * COLS)
        l_ref[:, cols] = jnp.where(
            sub8 == 0, blk[r : r + 1], jnp.where(sub8 == 1, low[r : r + 1], jnp.where(sub8 == 2, 1.0, 0.0))
        )
        b_ref[cols, :] = hot_across(within[:, r : r + 1])
        pair_ref[:, cols] = jnp.broadcast_to(pair[r : r + 1], (16, COLS)).astype(BF16)

    for copy in arriving:
        copy.wait()
    t_ref[...] = temp_in[...].astype(F32)
    h_ref[...] = humid_in[...].astype(F32)
    for r in range(ROWS):
        cols = slice(r * COLS, (r + 1) * COLS)
        x_ref[0:LEV, cols] = t_ref[:, r, :].astype(BF16)
        x_ref[LEV : 2 * LEV, cols] = h_ref[:, r, :].astype(BF16)

    values = x_ref[...].reshape(VALUES // 16, 16, CELLS)
    labels = l_ref[...]
    leaving = []
    for step in range(PAIRS // GROUP):
        chosen = []
        extra = []
        for j in range(GROUP):
            p = step * GROUP + j
            mask = pair_ref[...] == jnp.asarray(p, BF16)
            chosen.append(jnp.where(mask[None], values, jnp.zeros_like(values)).reshape(VALUES, CELLS))
            extra.append(jnp.where(pair_ref[0:8, :].astype(F32) == float(p), labels, 0.0))
        chosen.append(jnp.concatenate(extra, axis=0).astype(BF16))
        moved = jnp.dot(jnp.concatenate(chosen, axis=0), b_ref[...], preferred_element_type=F32).astype(BF16)
        for j in range(GROUP):
            p = step * GROUP + j
            part = moved[j * VALUES : (j + 1) * VALUES]
            label = moved[GROUP * VALUES + 8 * j : GROUP * VALUES + 8 * (j + 1)]
            for h in range(2):
                send_out[2 * p + h, 0:VALUES, :] = part[:, h * CAP : (h + 1) * CAP]
                send_out[2 * p + h, VALUES:SEND, :] = label[:, h * CAP : (h + 1) * CAP]
        done = pl.ds(2 * step * GROUP, 2 * GROUP)
        copy = pltpu.make_async_copy(send_out.at[done], send_ref.at[done], out_sem.at[step])
        copy.start()
        leaving.append(copy)
    for copy in leaving:
        copy.wait()


def pack(temp, humid, parent):
    vmem = pl.BlockSpec(memory_space=pltpu.VMEM)
    hbm = pl.BlockSpec(memory_space=pltpu.HBM)
    field = (LEV, ROWS, COLS)
    return pl.pallas_call(
        pack_kernel,
        out_shape=(
            pltpu.HBM((TILES, SEND, CAP), BF16),
            pltpu.VMEM((ROWS, COLS), jnp.int32),
        ),
        in_specs=[hbm, hbm, hbm],
        out_specs=(hbm, vmem),
        scratch_shapes=[
            pltpu.VMEM(field, BF16),
            pltpu.VMEM(field, BF16),
            pltpu.VMEM((ROWS, COLS), jnp.int32),
            pltpu.VMEM((TILES, SEND, CAP), BF16),
            pltpu.VMEM(field, F32),
            pltpu.VMEM(field, F32),
            pltpu.VMEM((VALUES, CELLS), BF16),
            pltpu.VMEM((8, CELLS), F32),
            pltpu.VMEM((CELLS, COLS), BF16),
            pltpu.VMEM((16, CELLS), BF16),
            pltpu.SemaphoreType.DMA((3,)),
            pltpu.SemaphoreType.DMA((PAIRS // GROUP,)),
        ],
        compiler_params=pltpu.CompilerParams(vmem_limit_bytes=VMEM),
    )(
        pltpu.with_memory_space_constraint(temp, pltpu.HBM),
        pltpu.with_memory_space_constraint(humid, pltpu.HBM),
        pltpu.with_memory_space_constraint(parent, pltpu.HBM),
    )


def hot_down(row):
    n = row.shape[1]
    index = lax.broadcasted_iota(jnp.int32, (256, n), 0).astype(F32).astype(BF16).reshape(16, 16, n)
    hit = index == jnp.broadcast_to(row, (16, n)).astype(BF16)[None]
    return jnp.where(hit, jnp.ones_like(index), jnp.zeros_like(index)).reshape(256, n)


def hot_across(column):
    n = column.shape[0]
    index = lax.broadcasted_iota(jnp.int32, (n, 256), 1).astype(F32).astype(BF16)
    hit = index == jnp.broadcast_to(column, (n, 256))
    return jnp.where(hit, jnp.ones_like(index), jnp.zeros_like(index))


def owner_kernel(recv_ref, kabs_in, planck_ref, top_ref, out_ref,
                 kabs_ref, kabs_sem, b_ref, absorb_ref, emit_ref, step_ref, hmean_ref, net_ref, trans_ref, rise_ref, sum_ref, q_ref,
                 answer_ref, out_sem):
    arriving = pltpu.make_async_copy(kabs_in, kabs_ref, kabs_sem)
    arriving.start()
    lows = jnp.concatenate([recv_ref[s, BLK_ROW:SEND, :].astype(F32)[1:2] for s in range(TILES)], axis=0)
    low_cols = lows.T.astype(BF16)

    for first in range(0, TILES, 4):
        lhs = []
        rhs = []
        for s in range(first, first + 4):
            got = recv_ref[s]
            blk = jnp.broadcast_to(got[BLK_ROW:SEND].astype(F32)[0:1], (SEND, CAP)).astype(BF16)
            half = slice((s % 2) * CAP, (s % 2 + 1) * CAP)
            b_ref[s // 2, :, half] = hot_down(lows[s : s + 1])
            rhs.append(hot_across(low_cols[:, s : s + 1]))
            zero = jnp.zeros_like(got)
            lhs.append(
                jnp.concatenate([jnp.where(blk == jnp.asarray(b + 1, BF16), got, zero) for b in range(4)], axis=0)
            )
        part = jnp.dot(
            jnp.concatenate(lhs, axis=1), jnp.concatenate(rhs, axis=0), preferred_element_type=F32
        )
        if first == 0:
            sum_ref[...] = part
        else:
            sum_ref[...] += part

    counts = []
    for b in range(4):
        for h in range(2):
            lanes = slice(h * CAP, (h + 1) * CAP)
            row = b * SEND + ONE_ROW
            counts.append(sum_ref[row : row + 1, lanes])
            emit_ref[:, 2 * b + h, :] = sum_ref[b * SEND : b * SEND + LEV, lanes]
            hmean_ref[:, 2 * b + h, :] = sum_ref[b * SEND + LEV : b * SEND + 2 * LEV, lanes]
    inv = 1.0 / jnp.maximum(jnp.concatenate(counts, axis=0), 1.0)
    hc = hmean_ref[...] * inv[None]
    absorb_ref[...] = jnp.exp(0.5 * hc)
    emit = jnp.exp(0.25 * (emit_ref[...] * inv[None]))
    emit_ref[...] = emit
    step_ref[0 : LEV - 1] = emit[1:LEV] - emit[0 : LEV - 1]
    hmean_ref[...] = hc
    net_ref[...] = jnp.zeros_like(net_ref)
    emit_top = emit_ref[0]
    emit_low = emit_ref[LEV - 1]

    def one_block(block, top_net):
        first = block * GB
        tops = [top_ref[first + j] for j in range(GB)]
        planck = [planck_ref[first + j] for j in range(GB)]
        state = [tops[j] - emit_top * planck[j] for j in range(GB)]
        for k in range(LEV):
            absorb = absorb_ref[k]
            total = None
            for j in range(GB):
                t = jnp.exp2(absorb * kabs_ref[first + j, k])
                trans_ref[k, j] = t
                state[j] = t * state[j]
                total = state[j] if total is None else total + state[j]
            net_ref[k] += total
            if k < LEV - 1:
                step = step_ref[k]
                for j in range(GB):
                    rise = step * planck[j]
                    rise_ref[k, j] = rise
                    state[j] = state[j] - rise
        state = [
            0.3 * (state[j] + emit_low * planck[j]) - emit_low * planck[j] for j in range(GB)
        ]
        for k in range(LEV - 1, -1, -1):
            total = None
            for j in range(GB):
                state[j] = trans_ref[k, j] * state[j]
                total = state[j] if total is None else total + state[j]
            net_ref[k] -= total
            if k > 0:
                state = [state[j] + rise_ref[k - 1, j] for j in range(GB)]
        for j in range(GB):
            top_net = top_net + (tops[j] - (state[j] + emit_top * planck[j]))
        return top_net

    arriving.wait()
    top_net = lax.fori_loop(0, G // GB, one_block, jnp.zeros((8, 128), F32), unroll=2)
    net = net_ref[...]
    prev = jnp.concatenate([top_net[None], net[:-1]], axis=0)
    heat = ((prev - net) * (LEV / G)).astype(BF16).astype(F32)
    hm = hmean_ref[...].astype(BF16).astype(F32)
    net_ref[...] = heat - 0.5 * hm
    for b in range(4):
        for h in range(2):
            q_ref[b * LEV : (b + 1) * LEV, h * CAP : (h + 1) * CAP] = net_ref[:, 2 * b + h, :].astype(BF16)

    leaving = []
    for p in range(PAIRS):
        both = jnp.dot(q_ref[...], b_ref[p], preferred_element_type=F32)
        for h in range(2):
            lanes = slice(h * CAP, (h + 1) * CAP)
            blk = recv_ref[2 * p + h, BLK_ROW:SEND, :].astype(F32)[0:1]
            got = jnp.zeros((LEV, CAP), F32)
            for b in range(4):
                got = jnp.where(blk == float(b + 1), both[b * LEV : (b + 1) * LEV, lanes], got)
            answer_ref[2 * p + h] = got.astype(BF16)
        if p % (PAIRS // 4) == PAIRS // 4 - 1:
            step = p // (PAIRS // 4)
            done = pl.ds(step * (TILES // 4), TILES // 4)
            copy = pltpu.make_async_copy(answer_ref.at[done], out_ref.at[done], out_sem.at[step])
            copy.start()
            leaving.append(copy)
    for copy in leaving:
        copy.wait()


def owner_step(recv, kabs, planck, top_flux):
    column = pltpu.VMEM((LEV, 8, 128), F32)
    return call(
        owner_kernel,
        jax.ShapeDtypeStruct((TILES, LEV, CAP), BF16),
        (recv, kabs * (-LOG2E), planck, top_flux),
        [
            pltpu.SMEM((G, LEV), F32),
            pltpu.SemaphoreType.DMA,
            pltpu.VMEM((PAIRS, 256, 256), BF16),
            column,
            column,
            column,
            column,
            column,
            pltpu.VMEM((LEV, GB, 8, 128), F32),
            pltpu.VMEM((LEV, GB, 8, 128), F32),
            pltpu.VMEM((4 * SEND, 256), F32),
            pltpu.VMEM((4 * LEV, 256), BF16),
            pltpu.VMEM((TILES, LEV, CAP), BF16),
            pltpu.SemaphoreType.DMA((4,)),
        ],
        scalars=2,
        out_space=pltpu.HBM,
    )


def gather_columns(row_of):
    first = row_of(0)
    lane = lax.broadcasted_iota(jnp.int32, (first.shape[0], 128), 1)
    kept = jnp.zeros((first.shape[0], 128), first.dtype)
    for r in range(ROWS):
        row = row_of(r)
        kept = jnp.where(lane == r, row[:, 0:1], kept)
        kept = jnp.where(lane == ROWS + r, row[:, COLS - 1 : COLS], kept)
    return kept


def split_columns(columns):
    return columns.astype(BF16), pltpu.roll(columns, 128 - ROWS, axis=1).astype(BF16)


def edge_shapes():
    row = jax.ShapeDtypeStruct((LEV, COLS), BF16)
    column = jax.ShapeDtypeStruct((LEV, 128), BF16)
    return row, row, column, column


def edges_kernel(temp_ref, top_ref, bottom_ref, left_ref, right_ref, t_ref):
    t_ref[...] = temp_ref[...].astype(F32)
    top_ref[...] = t_ref[:, 0, :].astype(BF16)
    bottom_ref[...] = t_ref[:, ROWS - 1, :].astype(BF16)
    left_ref[...], right_ref[...] = split_columns(gather_columns(lambda r: t_ref[:, r, :]))


def edges(temp):
    return call(
        edges_kernel, edge_shapes(), (temp,), [pltpu.VMEM((LEV, ROWS, COLS), F32)], resident_in=False
    )


def stencil_row(value, above, below, left, right):
    lane = lax.broadcasted_iota(jnp.int32, value.shape, 1)
    west = jnp.where(lane == 0, left, pltpu.roll(value, 1, axis=1))
    east = jnp.where(lane == COLS - 1, right, pltpu.roll(value, COLS - 1, axis=1))
    return value + 0.2 * (above + below + west + east - 4.0 * value)


def stencil_rows(row_of, above_ref, below_ref, left_ref, right_ref):
    left = left_ref[...].astype(F32)
    right = right_ref[...].astype(F32)
    above = above_ref[...].astype(F32)
    value = row_of(0)
    for r in range(ROWS):
        below = row_of(r + 1) if r < ROWS - 1 else below_ref[...].astype(F32)
        yield r, stencil_row(value, above, below, left[:, r : r + 1], right[:, r : r + 1])
        above, value = value, below


def base_kernel(temp_ref, humid_ref, slot_ref, above_ref, below_ref, left_ref, right_ref,
                base_ref, base_cols_ref, slot_cols_ref, t_ref, h_ref):
    t_ref[...] = temp_ref[...].astype(F32)
    h_ref[...] = humid_ref[...].astype(F32)
    for r, first in stencil_rows(lambda r: t_ref[:, r, :], above_ref, below_ref, left_ref, right_ref):
        base_ref[r] = first.astype(BF16).astype(F32) + 0.25 * h_ref[:, r, :]
    base_cols_ref[...] = gather_columns(lambda r: base_ref[r])
    slot = slot_ref[...]
    slots = gather_columns(lambda r: slot[r : r + 1])
    slot_cols_ref[...] = jnp.broadcast_to(slots, (8, 128))


def base_step(temp, humid, slot, halo):
    return call(
        base_kernel,
        (
            jax.ShapeDtypeStruct((ROWS, LEV, COLS), F32),
            jax.ShapeDtypeStruct((LEV, 128), F32),
            jax.ShapeDtypeStruct((8, 128), jnp.int32),
        ),
        (temp, humid, slot, *halo),
        [pltpu.VMEM((LEV, ROWS, COLS), F32), pltpu.VMEM((LEV, ROWS, COLS), F32)],
    )


def in_pairs(ret_ref, r_ref):
    for p in range(PAIRS):
        for h in range(2):
            r_ref[p * LEV : (p + 1) * LEV, h * CAP : (h + 1) * CAP] = ret_ref[2 * p + h]


def picked(r_ref, slot):
    count = slot.shape[1]
    pair = slot // 256
    moved = jnp.dot(r_ref[...], hot_down((slot % 256).astype(F32)), preferred_element_type=F32)
    q = jnp.zeros((LEV, count), F32)
    for p in range(PAIRS):
        q = jnp.where(pair == p, moved[p * LEV : (p + 1) * LEV], q)
    return q


def rim_kernel(ret_ref, slot_ref, slot_cols_ref, base_ref, base_cols_ref,
               top_ref, bottom_ref, left_ref, right_ref, r_ref):
    in_pairs(ret_ref, r_ref)
    slot = jnp.concatenate(
        [slot_ref[0:1, :], slot_ref[ROWS - 1 : ROWS, :], slot_cols_ref[0:1, :]], axis=1
    )
    q = 0.5 * picked(r_ref, slot)
    top_ref[...] = (base_ref[0] + q[:, 0:COLS]).astype(BF16)
    bottom_ref[...] = (base_ref[ROWS - 1] + q[:, COLS : 2 * COLS]).astype(BF16)
    left_ref[...], right_ref[...] = split_columns(base_cols_ref[...] + q[:, 2 * COLS :])


def rim(ret, slot, slot_cols, base, base_cols):
    return call(
        rim_kernel,
        edge_shapes(),
        (ret, slot, slot_cols, base, base_cols),
        [pltpu.VMEM((PAIRS * LEV, 256), BF16)],
    )


def unpack_kernel(ret_ref, slot_ref, base_ref, top_ref, bottom_ref, second_ref, r_ref):
    in_pairs(ret_ref, r_ref)
    second_ref[0] = top_ref[...]
    second_ref[ROWS - 1] = bottom_ref[...]
    for r in range(1, ROWS - 1):
        q = picked(r_ref, slot_ref[r : r + 1, :])
        second_ref[r] = (base_ref[r] + 0.5 * q).astype(BF16)


def unpack(ret, slot, base, top, bottom):
    return call(
        unpack_kernel,
        jax.ShapeDtypeStruct((ROWS, LEV, COLS), BF16),
        (ret, slot, base, top, bottom),
        [pltpu.VMEM((PAIRS * LEV, 256), BF16)],
    )


def last_kernel(second_ref, above_ref, below_ref, left_ref, right_ref, out_ref, o_ref, whole_ref, out_sem):
    row_of = lambda r: second_ref[r].astype(F32)
    for r, value in stencil_rows(row_of, above_ref, below_ref, left_ref, right_ref):
        o_ref[:, r, :] = value
    leaving = []
    for step in range(4):
        done = pl.ds(step * (LEV // 4), LEV // 4)
        whole_ref[done] = o_ref[done].astype(BF16)
        copy = pltpu.make_async_copy(whole_ref.at[done], out_ref.at[done], out_sem.at[step])
        copy.start()
        leaving.append(copy)
    for copy in leaving:
        copy.wait()


def last_step(second, halo):
    field = (LEV, ROWS, COLS)
    return call(
        last_kernel,
        jax.ShapeDtypeStruct(field, BF16),
        (second, *halo),
        [pltpu.VMEM(field, F32), pltpu.VMEM(field, BF16), pltpu.SemaphoreType.DMA((4,))],
        out_space=pltpu.HBM,
    )


def exchange(top, bottom, left, right):
    grp = lax.axis_size("grp")
    tile = lax.axis_size("tile")
    up = [(i, (i + 1) % grp) for i in range(grp)]
    along = [(i, (i + 1) % tile) for i in range(tile)]
    above = lax.ppermute(bottom, "grp", up)
    below = lax.ppermute(top, "grp", [(b, a) for a, b in up])
    west = lax.ppermute(right, "tile", along)
    east = lax.ppermute(left, "tile", [(b, a) for a, b in along])
    return above, below, west, east


def on_device(temp, humid, parent, kabs, planck, top_flux):
    send, slot = pack(temp, humid, parent)
    recv = lax.all_to_all(send, "tile", split_axis=0, concat_axis=0, tiled=True)
    recv, halo = lax.optimization_barrier((recv, exchange(*edges(temp))))
    answer = owner_step(recv, kabs, planck, top_flux)
    answer, halo = lax.optimization_barrier((answer, halo))
    ret = lax.all_to_all(answer, "tile", split_axis=0, concat_axis=0, tiled=True)
    base, base_cols, slot_cols = base_step(temp, humid, slot, halo)
    top, bottom, left, right = rim(ret, slot, slot_cols, base, base_cols)
    halo = exchange(top, bottom, left, right)
    second = unpack(ret, slot, base, top, bottom)
    return last_step(second, halo)


def solution(mesh):
    placed = (P(None, "grp", "tile"), P(None, "grp", "tile"), P("grp", "tile"), P(), P(), P())
    return jax.shard_map(
        on_device, mesh=mesh, in_specs=placed, out_specs=P(None, "grp", "tile"), check_vma=False
    )
```

```python
import jax
import jax.numpy as jnp
from jax import lax
from jax.experimental import pallas as pl
from jax.experimental.pallas import tpu as pltpu
from jax.sharding import PartitionSpec as P

F32 = jnp.float32
BF16 = jnp.bfloat16
LEV = 48
G = 112
ROWS = 16
COLS = 256
CELLS = ROWS * COLS
OWNED = 1024
TILES = 64
CAP = 128
PAIRS = TILES // 2
BLK_ROW = 96
ONE_ROW = 98
SEND = 104
VALUES = 96
GROUP = 8
GB = 7
LOG2E = 1.4426950408889634
VMEM = 32 * 1024 * 1024


def call(kernel, out_shape, operands, scratch=(), scalars=0, resident_in=True, out_space=pltpu.VMEM):
    vmem = pl.BlockSpec(memory_space=pltpu.VMEM)
    smem = pl.BlockSpec(memory_space=pltpu.SMEM)
    many = isinstance(out_shape, tuple)
    arrays = len(operands) - scalars
    if resident_in:
        operands = [
            pltpu.with_memory_space_constraint(x, pltpu.VMEM) if i < arrays else x for i, x in enumerate(operands)
        ]
    if out_space is not None:
        place = lambda x: out_space(x.shape, x.dtype)
        out_shape = tuple(place(x) for x in out_shape) if many else place(out_shape)
    out = pl.BlockSpec(memory_space=pltpu.HBM if out_space is pltpu.HBM else pltpu.VMEM)
    return pl.pallas_call(
        kernel,
        out_shape=out_shape,
        in_specs=[vmem] * arrays + [smem] * scalars,
        out_specs=(out,) * len(out_shape) if many else out,
        scratch_shapes=list(scratch),
        compiler_params=pltpu.CompilerParams(vmem_limit_bytes=VMEM),
    )(*operands)


def pack_kernel(temp_ref, humid_ref, parent_ref, send_ref, slot_ref,
                temp_in, humid_in, parent_in, send_out, t_ref, h_ref, x_ref, l_ref, b_ref, pair_ref, in_sem, out_sem):
    arriving = [
        pltpu.make_async_copy(temp_ref, temp_in, in_sem.at[0]),
        pltpu.make_async_copy(humid_ref, humid_in, in_sem.at[1]),
    ]
    named = pltpu.make_async_copy(parent_ref, parent_in, in_sem.at[2])
    named.start()
    for copy in arriving:
        copy.start()
    sub = lax.broadcasted_iota(jnp.int32, (COLS, COLS), 0)
    lane = lax.broadcasted_iota(jnp.int32, (COLS, COLS), 1)
    before = (sub < lane).astype(BF16)
    ones = jnp.ones((COLS, COLS), BF16)
    sub64 = lax.broadcasted_iota(jnp.int32, (TILES, COLS), 0)
    sub8 = lax.broadcasted_iota(jnp.int32, (8, COLS), 0)
    named.wait()
    parent = parent_in[...]
    owner = parent // OWNED
    local = parent % OWNED
    blk = (local // 256 + 1).astype(F32)
    low = (local % 256).astype(F32)
    hits = [jnp.where(owner[r : r + 1] == sub64, 1.0, 0.0).astype(F32) for r in range(ROWS)]
    stacked = jnp.concatenate([h.astype(BF16) for h in hits], axis=0)
    ranks = jnp.dot(stacked, before, preferred_element_type=F32)
    totals = jnp.dot(stacked, ones, preferred_element_type=F32)
    carry = jnp.zeros((TILES, COLS), F32)
    position = []
    for r in range(ROWS):
        span = slice(r * TILES, (r + 1) * TILES)
        position.append(jnp.sum(hits[r] * (ranks[span] + carry), axis=0, keepdims=True))
        carry = carry + totals[span]
    slot = owner * CAP + jnp.concatenate(position, axis=0).astype(jnp.int32)
    slot_ref[...] = slot
    pair = (slot // 256).astype(F32)
    within = (slot % 256).astype(F32).T.astype(BF16)
    for r in range(ROWS):
        cols = slice(r * COLS, (r + 1) * COLS)
        l_ref[:, cols] = jnp.where(
            sub8 == 0, blk[r : r + 1], jnp.where(sub8 == 1, low[r : r + 1], jnp.where(sub8 == 2, 1.0, 0.0))
        )
        b_ref[cols, :] = hot_across(within[:, r : r + 1])
        pair_ref[:, cols] = jnp.broadcast_to(pair[r : r + 1], (16, COLS)).astype(BF16)

    for copy in arriving:
        copy.wait()
    t_ref[...] = temp_in[...].astype(F32)
    h_ref[...] = humid_in[...].astype(F32)
    for r in range(ROWS):
        cols = slice(r * COLS, (r + 1) * COLS)
        x_ref[0:LEV, cols] = t_ref[:, r, :].astype(BF16)
        x_ref[LEV : 2 * LEV, cols] = h_ref[:, r, :].astype(BF16)

    values = x_ref[...].reshape(VALUES // 16, 16, CELLS)
    labels = l_ref[...]
    leaving = []
    for step in range(PAIRS // GROUP):
        chosen = []
        extra = []
        for j in range(GROUP):
            p = step * GROUP + j
            mask = pair_ref[...] == jnp.asarray(p, BF16)
            chosen.append(jnp.where(mask[None], values, jnp.zeros_like(values)).reshape(VALUES, CELLS))
            extra.append(jnp.where(pair_ref[0:8, :].astype(F32) == float(p), labels, 0.0))
        chosen.append(jnp.concatenate(extra, axis=0).astype(BF16))
        moved = jnp.dot(jnp.concatenate(chosen, axis=0), b_ref[...], preferred_element_type=F32).astype(BF16)
        for j in range(GROUP):
            p = step * GROUP + j
            part = moved[j * VALUES : (j + 1) * VALUES]
            label = moved[GROUP * VALUES + 8 * j : GROUP * VALUES + 8 * (j + 1)]
            for h in range(2):
                send_out[2 * p + h, 0:VALUES, :] = part[:, h * CAP : (h + 1) * CAP]
                send_out[2 * p + h, VALUES:SEND, :] = label[:, h * CAP : (h + 1) * CAP]
        done = pl.ds(2 * step * GROUP, 2 * GROUP)
        copy = pltpu.make_async_copy(send_out.at[done], send_ref.at[done], out_sem.at[step])
        copy.start()
        leaving.append(copy)
    for copy in leaving:
        copy.wait()


def pack(temp, humid, parent):
    vmem = pl.BlockSpec(memory_space=pltpu.VMEM)
    hbm = pl.BlockSpec(memory_space=pltpu.HBM)
    field = (LEV, ROWS, COLS)
    return pl.pallas_call(
        pack_kernel,
        out_shape=(
            pltpu.HBM((TILES, SEND, CAP), BF16),
            pltpu.VMEM((ROWS, COLS), jnp.int32),
        ),
        in_specs=[hbm, hbm, hbm],
        out_specs=(hbm, vmem),
        scratch_shapes=[
            pltpu.VMEM(field, BF16),
            pltpu.VMEM(field, BF16),
            pltpu.VMEM((ROWS, COLS), jnp.int32),
            pltpu.VMEM((TILES, SEND, CAP), BF16),
            pltpu.VMEM(field, F32),
            pltpu.VMEM(field, F32),
            pltpu.VMEM((VALUES, CELLS), BF16),
            pltpu.VMEM((8, CELLS), F32),
            pltpu.VMEM((CELLS, COLS), BF16),
            pltpu.VMEM((16, CELLS), BF16),
            pltpu.SemaphoreType.DMA((3,)),
            pltpu.SemaphoreType.DMA((PAIRS // GROUP,)),
        ],
        compiler_params=pltpu.CompilerParams(vmem_limit_bytes=VMEM),
    )(
        pltpu.with_memory_space_constraint(temp, pltpu.HBM),
        pltpu.with_memory_space_constraint(humid, pltpu.HBM),
        pltpu.with_memory_space_constraint(parent, pltpu.HBM),
    )


def hot_down(row):
    n = row.shape[1]
    index = lax.broadcasted_iota(jnp.int32, (256, n), 0).astype(F32).astype(BF16).reshape(16, 16, n)
    hit = index == jnp.broadcast_to(row, (16, n)).astype(BF16)[None]
    return jnp.where(hit, jnp.ones_like(index), jnp.zeros_like(index)).reshape(256, n)


def hot_across(column):
    n = column.shape[0]
    index = lax.broadcasted_iota(jnp.int32, (n, 256), 1).astype(F32).astype(BF16)
    hit = index == jnp.broadcast_to(column, (n, 256))
    return jnp.where(hit, jnp.ones_like(index), jnp.zeros_like(index))


def owner_kernel(recv_ref, table_in, out_ref,
                 table_ref, table_sem, b_ref, absorb_ref, emit_ref, step_ref, hmean_ref, net_ref, trans_ref, rise_ref, sum_ref, q_ref,
                 answer_ref, out_sem):
    arriving = pltpu.make_async_copy(table_in, table_ref, table_sem)
    arriving.start()
    lows = jnp.concatenate([recv_ref[s, BLK_ROW:SEND, :].astype(F32)[1:2] for s in range(TILES)], axis=0)
    low_cols = lows.T.astype(BF16)

    for first in range(0, TILES, 4):
        lhs = []
        rhs = []
        for s in range(first, first + 4):
            got = recv_ref[s]
            blk = jnp.broadcast_to(got[BLK_ROW:SEND].astype(F32)[0:1], (SEND, CAP)).astype(BF16)
            half = slice((s % 2) * CAP, (s % 2 + 1) * CAP)
            b_ref[s // 2, :, half] = hot_down(lows[s : s + 1])
            rhs.append(hot_across(low_cols[:, s : s + 1]))
            zero = jnp.zeros_like(got)
            lhs.append(
                jnp.concatenate([jnp.where(blk == jnp.asarray(b + 1, BF16), got, zero) for b in range(4)], axis=0)
            )
        part = jnp.dot(
            jnp.concatenate(lhs, axis=1), jnp.concatenate(rhs, axis=0), preferred_element_type=F32
        )
        if first == 0:
            sum_ref[...] = part
        else:
            sum_ref[...] += part

    counts = []
    for b in range(4):
        for h in range(2):
            lanes = slice(h * CAP, (h + 1) * CAP)
            row = b * SEND + ONE_ROW
            counts.append(sum_ref[row : row + 1, lanes])
            emit_ref[:, 2 * b + h, :] = sum_ref[b * SEND : b * SEND + LEV, lanes]
            hmean_ref[:, 2 * b + h, :] = sum_ref[b * SEND + LEV : b * SEND + 2 * LEV, lanes]
    inv = 1.0 / jnp.maximum(jnp.concatenate(counts, axis=0), 1.0)
    hc = hmean_ref[...] * inv[None]
    absorb_ref[...] = jnp.exp(0.5 * hc)
    emit = jnp.exp(0.25 * (emit_ref[...] * inv[None]))
    emit_ref[...] = emit
    step_ref[0 : LEV - 1] = emit[1:LEV] - emit[0 : LEV - 1]
    hmean_ref[...] = hc
    net_ref[...] = jnp.zeros_like(net_ref)
    emit_top = emit_ref[0]
    emit_low = emit_ref[LEV - 1]

    def one_block(block, top_net):
        first = block * GB
        tops = [table_ref[first + j, LEV + 1] for j in range(GB)]
        planck = [table_ref[first + j, LEV] for j in range(GB)]
        state = [tops[j] - emit_top * planck[j] for j in range(GB)]
        for k in range(LEV):
            absorb = absorb_ref[k]
            total = None
            for j in range(GB):
                t = jnp.exp2(absorb * table_ref[first + j, k])
                trans_ref[k, j] = t
                state[j] = t * state[j]
                total = state[j] if total is None else total + state[j]
            net_ref[k] += total
            if k < LEV - 1:
                step = step_ref[k]
                for j in range(GB):
                    rise = step * planck[j]
                    rise_ref[k, j] = rise
                    state[j] = state[j] - rise
        state = [
            0.3 * (state[j] + emit_low * planck[j]) - emit_low * planck[j] for j in range(GB)
        ]
        for k in range(LEV - 1, -1, -1):
            total = None
            for j in range(GB):
                state[j] = trans_ref[k, j] * state[j]
                total = state[j] if total is None else total + state[j]
            net_ref[k] -= total
            if k > 0:
                state = [state[j] + rise_ref[k - 1, j] for j in range(GB)]
        for j in range(GB):
            top_net = top_net + (tops[j] - (state[j] + emit_top * planck[j]))
        return top_net

    arriving.wait()
    top_net = lax.fori_loop(0, G // GB, one_block, jnp.zeros((8, 128), F32), unroll=2)
    net = net_ref[...]
    prev = jnp.concatenate([top_net[None], net[:-1]], axis=0)
    heat = ((prev - net) * (LEV / G)).astype(BF16).astype(F32)
    hm = hmean_ref[...].astype(BF16).astype(F32)
    net_ref[...] = heat - 0.5 * hm
    for b in range(4):
        for h in range(2):
            q_ref[b * LEV : (b + 1) * LEV, h * CAP : (h + 1) * CAP] = net_ref[:, 2 * b + h, :].astype(BF16)

    leaving = []
    for p in range(PAIRS):
        both = jnp.dot(q_ref[...], b_ref[p], preferred_element_type=F32)
        for h in range(2):
            lanes = slice(h * CAP, (h + 1) * CAP)
            blk = recv_ref[2 * p + h, BLK_ROW:SEND, :].astype(F32)[0:1]
            got = jnp.zeros((LEV, CAP), F32)
            for b in range(4):
                got = jnp.where(blk == float(b + 1), both[b * LEV : (b + 1) * LEV, lanes], got)
            answer_ref[2 * p + h] = got.astype(BF16)
        if p % (PAIRS // 4) == PAIRS // 4 - 1:
            step = p // (PAIRS // 4)
            done = pl.ds(step * (TILES // 4), TILES // 4)
            copy = pltpu.make_async_copy(answer_ref.at[done], out_ref.at[done], out_sem.at[step])
            copy.start()
            leaving.append(copy)
    for copy in leaving:
        copy.wait()


def owner_step(recv, kabs, planck, top_flux):
    column = pltpu.VMEM((LEV, 8, 128), F32)
    return call(
        owner_kernel,
        jax.ShapeDtypeStruct((TILES, LEV, CAP), BF16),
        (recv, jnp.concatenate([kabs * (-LOG2E), planck[:, None], top_flux[:, None]], axis=1)),
        [
            pltpu.SMEM((G, LEV + 2), F32),
            pltpu.SemaphoreType.DMA,
            pltpu.VMEM((PAIRS, 256, 256), BF16),
            column,
            column,
            column,
            column,
            column,
            pltpu.VMEM((LEV, GB, 8, 128), F32),
            pltpu.VMEM((LEV, GB, 8, 128), F32),
            pltpu.VMEM((4 * SEND, 256), F32),
            pltpu.VMEM((4 * LEV, 256), BF16),
            pltpu.VMEM((TILES, LEV, CAP), BF16),
            pltpu.SemaphoreType.DMA((4,)),
        ],
        out_space=pltpu.HBM,
    )


def gather_columns(row_of):
    first = row_of(0)
    lane = lax.broadcasted_iota(jnp.int32, (first.shape[0], 128), 1)
    kept = jnp.zeros((first.shape[0], 128), first.dtype)
    for r in range(ROWS):
        row = row_of(r)
        kept = jnp.where(lane == r, row[:, 0:1], kept)
        kept = jnp.where(lane == ROWS + r, row[:, COLS - 1 : COLS], kept)
    return kept


def split_columns(columns):
    return columns.astype(BF16), pltpu.roll(columns, 128 - ROWS, axis=1).astype(BF16)


def edge_shapes():
    row = jax.ShapeDtypeStruct((LEV, COLS), BF16)
    column = jax.ShapeDtypeStruct((LEV, 128), BF16)
    return row, row, column, column


def edges_kernel(temp_ref, top_ref, bottom_ref, left_ref, right_ref, t_ref):
    t_ref[...] = temp_ref[...].astype(F32)
    top_ref[...] = t_ref[:, 0, :].astype(BF16)
    bottom_ref[...] = t_ref[:, ROWS - 1, :].astype(BF16)
    left_ref[...], right_ref[...] = split_columns(gather_columns(lambda r: t_ref[:, r, :]))


def edges(temp):
    return call(
        edges_kernel, edge_shapes(), (temp,), [pltpu.VMEM((LEV, ROWS, COLS), F32)], resident_in=False
    )


def stencil_row(value, above, below, left, right):
    lane = lax.broadcasted_iota(jnp.int32, value.shape, 1)
    west = jnp.where(lane == 0, left, pltpu.roll(value, 1, axis=1))
    east = jnp.where(lane == COLS - 1, right, pltpu.roll(value, COLS - 1, axis=1))
    return value + 0.2 * (above + below + west + east - 4.0 * value)


def stencil_rows(row_of, above_ref, below_ref, left_ref, right_ref):
    left = left_ref[...].astype(F32)
    right = right_ref[...].astype(F32)
    above = above_ref[...].astype(F32)
    value = row_of(0)
    for r in range(ROWS):
        below = row_of(r + 1) if r < ROWS - 1 else below_ref[...].astype(F32)
        yield r, stencil_row(value, above, below, left[:, r : r + 1], right[:, r : r + 1])
        above, value = value, below


def base_kernel(temp_ref, humid_ref, slot_ref, above_ref, below_ref, left_ref, right_ref,
                base_ref, base_cols_ref, slot_cols_ref, t_ref, h_ref):
    t_ref[...] = temp_ref[...].astype(F32)
    h_ref[...] = humid_ref[...].astype(F32)
    for r, first in stencil_rows(lambda r: t_ref[:, r, :], above_ref, below_ref, left_ref, right_ref):
        base_ref[r] = first.astype(BF16).astype(F32) + 0.25 * h_ref[:, r, :]
    base_cols_ref[...] = gather_columns(lambda r: base_ref[r])
    slot = slot_ref[...]
    slots = gather_columns(lambda r: slot[r : r + 1])
    slot_cols_ref[...] = jnp.broadcast_to(slots, (8, 128))


def base_step(temp, humid, slot, halo):
    return call(
        base_kernel,
        (
            jax.ShapeDtypeStruct((ROWS, LEV, COLS), F32),
            jax.ShapeDtypeStruct((LEV, 128), F32),
            jax.ShapeDtypeStruct((8, 128), jnp.int32),
        ),
        (temp, humid, slot, *halo),
        [pltpu.VMEM((LEV, ROWS, COLS), F32), pltpu.VMEM((LEV, ROWS, COLS), F32)],
    )


def in_pairs(ret_ref, r_ref):
    for p in range(PAIRS):
        for h in range(2):
            r_ref[p * LEV : (p + 1) * LEV, h * CAP : (h + 1) * CAP] = ret_ref[2 * p + h]


def picked(r_ref, slot):
    count = slot.shape[1]
    pair = slot // 256
    moved = jnp.dot(r_ref[...], hot_down((slot % 256).astype(F32)), preferred_element_type=F32)
    q = jnp.zeros((LEV, count), F32)
    for p in range(PAIRS):
        q = jnp.where(pair == p, moved[p * LEV : (p + 1) * LEV], q)
    return q


def rim_kernel(ret_ref, slot_ref, slot_cols_ref, base_ref, base_cols_ref,
               top_ref, bottom_ref, left_ref, right_ref, r_ref):
    in_pairs(ret_ref, r_ref)
    slot = jnp.concatenate(
        [slot_ref[0:1, :], slot_ref[ROWS - 1 : ROWS, :], slot_cols_ref[0:1, :]], axis=1
    )
    q = 0.5 * picked(r_ref, slot)
    top_ref[...] = (base_ref[0] + q[:, 0:COLS]).astype(BF16)
    bottom_ref[...] = (base_ref[ROWS - 1] + q[:, COLS : 2 * COLS]).astype(BF16)
    left_ref[...], right_ref[...] = split_columns(base_cols_ref[...] + q[:, 2 * COLS :])


def rim(ret, slot, slot_cols, base, base_cols):
    return call(
        rim_kernel,
        edge_shapes(),
        (ret, slot, slot_cols, base, base_cols),
        [pltpu.VMEM((PAIRS * LEV, 256), BF16)],
    )


def unpack_kernel(ret_ref, slot_ref, base_ref, top_ref, bottom_ref, second_ref, r_ref):
    in_pairs(ret_ref, r_ref)
    second_ref[0] = top_ref[...]
    second_ref[ROWS - 1] = bottom_ref[...]
    for r in range(1, ROWS - 1):
        q = picked(r_ref, slot_ref[r : r + 1, :])
        second_ref[r] = (base_ref[r] + 0.5 * q).astype(BF16)


def unpack(ret, slot, base, top, bottom):
    return call(
        unpack_kernel,
        jax.ShapeDtypeStruct((ROWS, LEV, COLS), BF16),
        (ret, slot, base, top, bottom),
        [pltpu.VMEM((PAIRS * LEV, 256), BF16)],
    )


def last_kernel(second_ref, above_ref, below_ref, left_ref, right_ref, out_ref, o_ref, whole_ref, out_sem):
    row_of = lambda r: second_ref[r].astype(F32)
    for r, value in stencil_rows(row_of, above_ref, below_ref, left_ref, right_ref):
        o_ref[:, r, :] = value
    leaving = []
    for step in range(4):
        done = pl.ds(step * (LEV // 4), LEV // 4)
        whole_ref[done] = o_ref[done].astype(BF16)
        copy = pltpu.make_async_copy(whole_ref.at[done], out_ref.at[done], out_sem.at[step])
        copy.start()
        leaving.append(copy)
    for copy in leaving:
        copy.wait()


def last_step(second, halo):
    field = (LEV, ROWS, COLS)
    return call(
        last_kernel,
        jax.ShapeDtypeStruct(field, BF16),
        (second, *halo),
        [pltpu.VMEM(field, F32), pltpu.VMEM(field, BF16), pltpu.SemaphoreType.DMA((4,))],
        out_space=pltpu.HBM,
    )


def exchange(top, bottom, left, right):
    grp = lax.axis_size("grp")
    tile = lax.axis_size("tile")
    up = [(i, (i + 1) % grp) for i in range(grp)]
    along = [(i, (i + 1) % tile) for i in range(tile)]
    above = lax.ppermute(bottom, "grp", up)
    below = lax.ppermute(top, "grp", [(b, a) for a, b in up])
    west = lax.ppermute(right, "tile", along)
    east = lax.ppermute(left, "tile", [(b, a) for a, b in along])
    return above, below, west, east


def on_device(temp, humid, parent, kabs, planck, top_flux):
    send, slot = pack(temp, humid, parent)
    recv = lax.all_to_all(send, "tile", split_axis=0, concat_axis=0, tiled=True)
    recv, halo = lax.optimization_barrier((recv, exchange(*edges(temp))))
    answer = owner_step(recv, kabs, planck, top_flux)
    answer, halo = lax.optimization_barrier((answer, halo))
    ret = lax.all_to_all(answer, "tile", split_axis=0, concat_axis=0, tiled=True)
    base, base_cols, slot_cols = base_step(temp, humid, slot, halo)
    top, bottom, left, right = rim(ret, slot, slot_cols, base, base_cols)
    halo = exchange(top, bottom, left, right)
    second = unpack(ret, slot, base, top, bottom)
    return last_step(second, halo)


def solution(mesh):
    placed = (P(None, "grp", "tile"), P(None, "grp", "tile"), P("grp", "tile"), P(), P(), P())
    return jax.shard_map(
        on_device, mesh=mesh, in_specs=placed, out_specs=P(None, "grp", "tile"), check_vma=False
    )
```

```python
import jax
import jax.numpy as jnp
from jax import lax
from jax.experimental import pallas as pl
from jax.experimental.pallas import tpu as pltpu
from jax.sharding import PartitionSpec as P

F32 = jnp.float32
BF16 = jnp.bfloat16
LEV = 48
G = 112
ROWS = 16
COLS = 256
CELLS = ROWS * COLS
OWNED = 1024
TILES = 64
CAP = 128
PAIRS = TILES // 2
BLK_ROW = 96
ONE_ROW = 98
SEND = 104
VALUES = 96
GROUP = 8
GB = 7
LOG2E = 1.4426950408889634
VMEM = 32 * 1024 * 1024


def call(kernel, out_shape, operands, scratch=(), scalars=0, resident_in=True, out_space=pltpu.VMEM):
    vmem = pl.BlockSpec(memory_space=pltpu.VMEM)
    smem = pl.BlockSpec(memory_space=pltpu.SMEM)
    many = isinstance(out_shape, tuple)
    arrays = len(operands) - scalars
    if resident_in:
        operands = [
            pltpu.with_memory_space_constraint(x, pltpu.VMEM) if i < arrays else x for i, x in enumerate(operands)
        ]
    if out_space is not None:
        place = lambda x: out_space(x.shape, x.dtype)
        out_shape = tuple(place(x) for x in out_shape) if many else place(out_shape)
    out = pl.BlockSpec(memory_space=pltpu.HBM if out_space is pltpu.HBM else pltpu.VMEM)
    return pl.pallas_call(
        kernel,
        out_shape=out_shape,
        in_specs=[vmem] * arrays + [smem] * scalars,
        out_specs=(out,) * len(out_shape) if many else out,
        scratch_shapes=list(scratch),
        compiler_params=pltpu.CompilerParams(vmem_limit_bytes=VMEM),
    )(*operands)


def pack_kernel(temp_ref, humid_ref, parent_ref, send_ref, slot_ref,
                temp_in, humid_in, parent_in, send_out, t_ref, h_ref, x_ref, l_ref, b_ref, pair_ref, in_sem, out_sem):
    arriving = [
        pltpu.make_async_copy(temp_ref, temp_in, in_sem.at[0]),
        pltpu.make_async_copy(humid_ref, humid_in, in_sem.at[1]),
    ]
    named = pltpu.make_async_copy(parent_ref, parent_in, in_sem.at[2])
    named.start()
    for copy in arriving:
        copy.start()
    sub = lax.broadcasted_iota(jnp.int32, (COLS, COLS), 0)
    lane = lax.broadcasted_iota(jnp.int32, (COLS, COLS), 1)
    before = (sub < lane).astype(BF16)
    ones = jnp.ones((COLS, COLS), BF16)
    sub64 = lax.broadcasted_iota(jnp.int32, (TILES, COLS), 0)
    sub8 = lax.broadcasted_iota(jnp.int32, (8, COLS), 0)
    named.wait()
    parent = parent_in[...]
    owner = parent // OWNED
    local = parent % OWNED
    blk = (local // 256 + 1).astype(F32)
    low = (local % 256).astype(F32)
    hits = [jnp.where(owner[r : r + 1] == sub64, 1.0, 0.0).astype(F32) for r in range(ROWS)]
    stacked = jnp.concatenate([h.astype(BF16) for h in hits], axis=0)
    ranks = jnp.dot(stacked, before, preferred_element_type=F32)
    totals = jnp.dot(stacked, ones, preferred_element_type=F32)
    carry = jnp.zeros((TILES, COLS), F32)
    position = []
    for r in range(ROWS):
        span = slice(r * TILES, (r + 1) * TILES)
        position.append(jnp.sum(hits[r] * (ranks[span] + carry), axis=0, keepdims=True))
        carry = carry + totals[span]
    slot = owner * CAP + jnp.concatenate(position, axis=0).astype(jnp.int32)
    slot_ref[...] = slot
    pair = (slot // 256).astype(F32)
    within = (slot % 256).astype(F32).T.astype(BF16)
    for r in range(ROWS):
        cols = slice(r * COLS, (r + 1) * COLS)
        l_ref[:, cols] = jnp.where(
            sub8 == 0, blk[r : r + 1], jnp.where(sub8 == 1, low[r : r + 1], jnp.where(sub8 == 2, 1.0, 0.0))
        )
        b_ref[cols, :] = hot_across(within[:, r : r + 1])
        pair_ref[:, cols] = jnp.broadcast_to(pair[r : r + 1], (16, COLS)).astype(BF16)

    for copy in arriving:
        copy.wait()
    t_ref[...] = temp_in[...].astype(F32)
    h_ref[...] = humid_in[...].astype(F32)
    for r in range(ROWS):
        cols = slice(r * COLS, (r + 1) * COLS)
        x_ref[0:LEV, cols] = t_ref[:, r, :].astype(BF16)
        x_ref[LEV : 2 * LEV, cols] = h_ref[:, r, :].astype(BF16)

    values = x_ref[...].reshape(VALUES // 16, 16, CELLS)
    labels = l_ref[...]
    leaving = []
    for step in range(PAIRS // GROUP):
        chosen = []
        extra = []
        for j in range(GROUP):
            p = step * GROUP + j
            mask = pair_ref[...] == jnp.asarray(p, BF16)
            chosen.append(jnp.where(mask[None], values, jnp.zeros_like(values)).reshape(VALUES, CELLS))
            extra.append(jnp.where(pair_ref[0:8, :].astype(F32) == float(p), labels, 0.0))
        chosen.append(jnp.concatenate(extra, axis=0).astype(BF16))
        moved = jnp.dot(jnp.concatenate(chosen, axis=0), b_ref[...], preferred_element_type=F32).astype(BF16)
        for j in range(GROUP):
            p = step * GROUP + j
            part = moved[j * VALUES : (j + 1) * VALUES]
            label = moved[GROUP * VALUES + 8 * j : GROUP * VALUES + 8 * (j + 1)]
            for h in range(2):
                send_out[2 * p + h, 0:VALUES, :] = part[:, h * CAP : (h + 1) * CAP]
                send_out[2 * p + h, VALUES:SEND, :] = label[:, h * CAP : (h + 1) * CAP]
        done = pl.ds(2 * step * GROUP, 2 * GROUP)
        copy = pltpu.make_async_copy(send_out.at[done], send_ref.at[done], out_sem.at[step])
        copy.start()
        leaving.append(copy)
    for copy in leaving:
        copy.wait()


def pack(temp, humid, parent):
    vmem = pl.BlockSpec(memory_space=pltpu.VMEM)
    hbm = pl.BlockSpec(memory_space=pltpu.HBM)
    field = (LEV, ROWS, COLS)
    return pl.pallas_call(
        pack_kernel,
        out_shape=(
            pltpu.HBM((TILES, SEND, CAP), BF16),
            pltpu.VMEM((ROWS, COLS), jnp.int32),
        ),
        in_specs=[hbm, hbm, hbm],
        out_specs=(hbm, vmem),
        scratch_shapes=[
            pltpu.VMEM(field, BF16),
            pltpu.VMEM(field, BF16),
            pltpu.VMEM((ROWS, COLS), jnp.int32),
            pltpu.VMEM((TILES, SEND, CAP), BF16),
            pltpu.VMEM(field, F32),
            pltpu.VMEM(field, F32),
            pltpu.VMEM((VALUES, CELLS), BF16),
            pltpu.VMEM((8, CELLS), F32),
            pltpu.VMEM((CELLS, COLS), BF16),
            pltpu.VMEM((16, CELLS), BF16),
            pltpu.SemaphoreType.DMA((3,)),
            pltpu.SemaphoreType.DMA((PAIRS // GROUP,)),
        ],
        compiler_params=pltpu.CompilerParams(vmem_limit_bytes=VMEM),
    )(
        pltpu.with_memory_space_constraint(temp, pltpu.HBM),
        pltpu.with_memory_space_constraint(humid, pltpu.HBM),
        pltpu.with_memory_space_constraint(parent, pltpu.HBM),
    )


def hot_down(row):
    n = row.shape[1]
    index = lax.broadcasted_iota(jnp.int32, (256, n), 0).astype(F32).astype(BF16).reshape(16, 16, n)
    hit = index == jnp.broadcast_to(row, (16, n)).astype(BF16)[None]
    return jnp.where(hit, jnp.ones_like(index), jnp.zeros_like(index)).reshape(256, n)


def hot_across(column):
    n = column.shape[0]
    index = lax.broadcasted_iota(jnp.int32, (n, 256), 1).astype(F32).astype(BF16)
    hit = index == jnp.broadcast_to(column, (n, 256))
    return jnp.where(hit, jnp.ones_like(index), jnp.zeros_like(index))


def owner_kernel(recv_ref, table_in, out_ref,
                 table_ref, table_sem, b_ref, absorb_ref, emit_ref, step_ref, hmean_ref, net_ref, trans_ref, rise_ref, sum_ref, q_ref,
                 answer_ref, out_sem):
    arriving = pltpu.make_async_copy(table_in, table_ref, table_sem)
    arriving.start()
    lows = jnp.concatenate([recv_ref[s, BLK_ROW:SEND, :].astype(F32)[1:2] for s in range(TILES)], axis=0)
    low_cols = lows.T.astype(BF16)

    for first in range(0, TILES, 4):
        lhs = []
        rhs = []
        for s in range(first, first + 4):
            got = recv_ref[s]
            blk = jnp.broadcast_to(got[BLK_ROW:SEND].astype(F32)[0:1], (SEND, CAP)).astype(BF16)
            half = slice((s % 2) * CAP, (s % 2 + 1) * CAP)
            b_ref[s // 2, :, half] = hot_down(lows[s : s + 1])
            rhs.append(hot_across(low_cols[:, s : s + 1]))
            zero = jnp.zeros_like(got)
            lhs.append(
                jnp.concatenate([jnp.where(blk == jnp.asarray(b + 1, BF16), got, zero) for b in range(4)], axis=0)
            )
        part = jnp.dot(
            jnp.concatenate(lhs, axis=1), jnp.concatenate(rhs, axis=0), preferred_element_type=F32
        )
        if first == 0:
            sum_ref[...] = part
        else:
            sum_ref[...] += part

    counts = []
    for b in range(4):
        for h in range(2):
            lanes = slice(h * CAP, (h + 1) * CAP)
            row = b * SEND + ONE_ROW
            counts.append(sum_ref[row : row + 1, lanes])
            emit_ref[:, 2 * b + h, :] = sum_ref[b * SEND : b * SEND + LEV, lanes]
            hmean_ref[:, 2 * b + h, :] = sum_ref[b * SEND + LEV : b * SEND + 2 * LEV, lanes]
    inv = 1.0 / jnp.maximum(jnp.concatenate(counts, axis=0), 1.0)
    hc = hmean_ref[...] * inv[None]
    absorb_ref[...] = jnp.exp(0.5 * hc)
    emit = jnp.exp(0.25 * (emit_ref[...] * inv[None]))
    emit_ref[...] = emit
    step_ref[0 : LEV - 1] = emit[1:LEV] - emit[0 : LEV - 1]
    hmean_ref[...] = hc
    net_ref[...] = jnp.zeros_like(net_ref)
    emit_top = emit_ref[0]
    emit_low = emit_ref[LEV - 1]

    def one_block(block, top_net):
        first = block * GB
        tops = [table_ref[first + j, LEV + 1] for j in range(GB)]
        planck = [table_ref[first + j, LEV] for j in range(GB)]
        state = [tops[j] - emit_top * planck[j] for j in range(GB)]
        for k in range(LEV):
            absorb = absorb_ref[k]
            total = None
            for j in range(GB):
                t = jnp.exp2(absorb * table_ref[first + j, k])
                trans_ref[k, j] = t
                state[j] = t * state[j]
                total = state[j] if total is None else total + state[j]
            net_ref[k] += total
            if k < LEV - 1:
                step = step_ref[k]
                for j in range(GB):
                    rise = step * planck[j]
                    rise_ref[k, j] = rise
                    state[j] = state[j] - rise
        state = [
            0.3 * (state[j] + emit_low * planck[j]) - emit_low * planck[j] for j in range(GB)
        ]
        for k in range(LEV - 1, -1, -1):
            total = None
            for j in range(GB):
                state[j] = trans_ref[k, j] * state[j]
                total = state[j] if total is None else total + state[j]
            net_ref[k] -= total
            if k > 0:
                state = [state[j] + rise_ref[k - 1, j] for j in range(GB)]
        for j in range(GB):
            top_net = top_net + (tops[j] - (state[j] + emit_top * planck[j]))
        return top_net

    arriving.wait()
    top_net = lax.fori_loop(0, G // GB, one_block, jnp.zeros((8, 128), F32), unroll=2)
    net = net_ref[...]
    prev = jnp.concatenate([top_net[None], net[:-1]], axis=0)
    heat = ((prev - net) * (LEV / G)).astype(BF16).astype(F32)
    hm = hmean_ref[...].astype(BF16).astype(F32)
    net_ref[...] = heat - 0.5 * hm
    for b in range(4):
        for h in range(2):
            q_ref[b * LEV : (b + 1) * LEV, h * CAP : (h + 1) * CAP] = net_ref[:, 2 * b + h, :].astype(BF16)

    leaving = []
    for p in range(PAIRS):
        both = jnp.dot(q_ref[...], b_ref[p], preferred_element_type=F32)
        for h in range(2):
            lanes = slice(h * CAP, (h + 1) * CAP)
            blk = recv_ref[2 * p + h, BLK_ROW:SEND, :].astype(F32)[0:1]
            got = jnp.zeros((LEV, CAP), F32)
            for b in range(4):
                got = jnp.where(blk == float(b + 1), both[b * LEV : (b + 1) * LEV, lanes], got)
            answer_ref[2 * p + h] = got.astype(BF16)
        if p % (PAIRS // 4) == PAIRS // 4 - 1:
            step = p // (PAIRS // 4)
            done = pl.ds(step * (TILES // 4), TILES // 4)
            copy = pltpu.make_async_copy(answer_ref.at[done], out_ref.at[done], out_sem.at[step])
            copy.start()
            leaving.append(copy)
    for copy in leaving:
        copy.wait()


def owner_step(recv, kabs, planck, top_flux):
    column = pltpu.VMEM((LEV, 8, 128), F32)
    return call(
        owner_kernel,
        jax.ShapeDtypeStruct((TILES, LEV, CAP), BF16),
        (recv, jnp.concatenate([kabs * (-LOG2E), planck[:, None], top_flux[:, None]], axis=1)),
        [
            pltpu.SMEM((G, LEV + 2), F32),
            pltpu.SemaphoreType.DMA,
            pltpu.VMEM((PAIRS, 256, 256), BF16),
            column,
            column,
            column,
            column,
            column,
            pltpu.VMEM((LEV, GB, 8, 128), F32),
            pltpu.VMEM((LEV, GB, 8, 128), F32),
            pltpu.VMEM((4 * SEND, 256), F32),
            pltpu.VMEM((4 * LEV, 256), BF16),
            pltpu.VMEM((TILES, LEV, CAP), BF16),
            pltpu.SemaphoreType.DMA((4,)),
        ],
        out_space=pltpu.HBM,
    )


def gather_columns(row_of):
    first = row_of(0)
    lane = lax.broadcasted_iota(jnp.int32, (first.shape[0], 128), 1)
    kept = jnp.zeros((first.shape[0], 128), first.dtype)
    for r in range(ROWS):
        row = row_of(r)
        kept = jnp.where(lane == r, row[:, 0:1], kept)
        kept = jnp.where(lane == ROWS + r, row[:, COLS - 1 : COLS], kept)
    return kept


def split_columns(columns):
    return columns.astype(BF16), pltpu.roll(columns, 128 - ROWS, axis=1).astype(BF16)


def edge_shapes():
    row = jax.ShapeDtypeStruct((LEV, COLS), BF16)
    column = jax.ShapeDtypeStruct((LEV, 128), BF16)
    return row, row, column, column


def edges_kernel(temp_ref, top_ref, bottom_ref, left_ref, right_ref, t_ref):
    t_ref[...] = temp_ref[...].astype(F32)
    top_ref[...] = t_ref[:, 0, :].astype(BF16)
    bottom_ref[...] = t_ref[:, ROWS - 1, :].astype(BF16)
    left_ref[...], right_ref[...] = split_columns(gather_columns(lambda r: t_ref[:, r, :]))


def edges(temp):
    return call(
        edges_kernel, edge_shapes(), (temp,), [pltpu.VMEM((LEV, ROWS, COLS), F32)], resident_in=False
    )


def stencil_row(value, above, below, left, right):
    lane = lax.broadcasted_iota(jnp.int32, value.shape, 1)
    west = jnp.where(lane == 0, left, pltpu.roll(value, 1, axis=1))
    east = jnp.where(lane == COLS - 1, right, pltpu.roll(value, COLS - 1, axis=1))
    return value + 0.2 * (above + below + west + east - 4.0 * value)


def stencil_rows(row_of, above_ref, below_ref, left_ref, right_ref):
    left = left_ref[...].astype(F32)
    right = right_ref[...].astype(F32)
    above = above_ref[...].astype(F32)
    value = row_of(0)
    for r in range(ROWS):
        below = row_of(r + 1) if r < ROWS - 1 else below_ref[...].astype(F32)
        yield r, stencil_row(value, above, below, left[:, r : r + 1], right[:, r : r + 1])
        above, value = value, below


def base_kernel(temp_ref, humid_ref, slot_ref, above_ref, below_ref, left_ref, right_ref,
                base_ref, base_cols_ref, slot_cols_ref, hot_ref, hot_cols_ref, t_ref, h_ref):
    t_ref[...] = temp_ref[...].astype(F32)
    h_ref[...] = humid_ref[...].astype(F32)
    for r, first in stencil_rows(lambda r: t_ref[:, r, :], above_ref, below_ref, left_ref, right_ref):
        base_ref[r] = first.astype(BF16).astype(F32) + 0.25 * h_ref[:, r, :]
    base_cols_ref[...] = gather_columns(lambda r: base_ref[r])
    slot = slot_ref[...]
    slots = gather_columns(lambda r: slot[r : r + 1])
    slot_cols_ref[...] = jnp.broadcast_to(slots, (8, 128))
    hot_cols_ref[...] = hot_down((slots % 256).astype(F32))
    for r in range(ROWS):
        hot_ref[r] = hot_down((slot[r : r + 1] % 256).astype(F32))


def base_step(temp, humid, slot, halo):
    return call(
        base_kernel,
        (
            jax.ShapeDtypeStruct((ROWS, LEV, COLS), F32),
            jax.ShapeDtypeStruct((LEV, 128), F32),
            jax.ShapeDtypeStruct((8, 128), jnp.int32),
            jax.ShapeDtypeStruct((ROWS, 256, COLS), BF16),
            jax.ShapeDtypeStruct((256, 128), BF16),
        ),
        (temp, humid, slot, *halo),
        [pltpu.VMEM((LEV, ROWS, COLS), F32), pltpu.VMEM((LEV, ROWS, COLS), F32)],
    )


def in_pairs(ret_ref, r_ref):
    for p in range(PAIRS):
        for h in range(2):
            r_ref[p * LEV : (p + 1) * LEV, h * CAP : (h + 1) * CAP] = ret_ref[2 * p + h]


def picked(r_ref, slot, hot):
    count = slot.shape[1]
    pair = slot // 256
    moved = jnp.dot(r_ref[...], hot, preferred_element_type=F32)
    q = jnp.zeros((LEV, count), F32)
    for p in range(PAIRS):
        q = jnp.where(pair == p, moved[p * LEV : (p + 1) * LEV], q)
    return q


def rim_kernel(ret_ref, slot_ref, slot_cols_ref, base_ref, base_cols_ref, hot_ref, hot_cols_ref,
               top_ref, bottom_ref, left_ref, right_ref, r_ref):
    in_pairs(ret_ref, r_ref)
    slot = jnp.concatenate(
        [slot_ref[0:1, :], slot_ref[ROWS - 1 : ROWS, :], slot_cols_ref[0:1, :]], axis=1
    )
    hot = jnp.concatenate([hot_ref[0], hot_ref[ROWS - 1], hot_cols_ref[...]], axis=1)
    q = 0.5 * picked(r_ref, slot, hot)
    top_ref[...] = (base_ref[0] + q[:, 0:COLS]).astype(BF16)
    bottom_ref[...] = (base_ref[ROWS - 1] + q[:, COLS : 2 * COLS]).astype(BF16)
    left_ref[...], right_ref[...] = split_columns(base_cols_ref[...] + q[:, 2 * COLS :])


def rim(ret, slot, slot_cols, base, base_cols, hot, hot_cols):
    return call(
        rim_kernel,
        edge_shapes(),
        (ret, slot, slot_cols, base, base_cols, hot, hot_cols),
        [pltpu.VMEM((PAIRS * LEV, 256), BF16)],
    )


def unpack_kernel(ret_ref, slot_ref, hot_ref, base_ref, top_ref, bottom_ref, second_ref, r_ref):
    in_pairs(ret_ref, r_ref)
    second_ref[0] = top_ref[...]
    second_ref[ROWS - 1] = bottom_ref[...]
    for r in range(1, ROWS - 1):
        q = picked(r_ref, slot_ref[r : r + 1, :], hot_ref[r])
        second_ref[r] = (base_ref[r] + 0.5 * q).astype(BF16)


def unpack(ret, slot, hot, base, top, bottom):
    return call(
        unpack_kernel,
        jax.ShapeDtypeStruct((ROWS, LEV, COLS), BF16),
        (ret, slot, hot, base, top, bottom),
        [pltpu.VMEM((PAIRS * LEV, 256), BF16)],
    )


def last_kernel(second_ref, above_ref, below_ref, left_ref, right_ref, out_ref, o_ref, whole_ref, out_sem):
    row_of = lambda r: second_ref[r].astype(F32)
    for r, value in stencil_rows(row_of, above_ref, below_ref, left_ref, right_ref):
        o_ref[:, r, :] = value
    leaving = []
    for step in range(4):
        done = pl.ds(step * (LEV // 4), LEV // 4)
        whole_ref[done] = o_ref[done].astype(BF16)
        copy = pltpu.make_async_copy(whole_ref.at[done], out_ref.at[done], out_sem.at[step])
        copy.start()
        leaving.append(copy)
    for copy in leaving:
        copy.wait()


def last_step(second, halo):
    field = (LEV, ROWS, COLS)
    return call(
        last_kernel,
        jax.ShapeDtypeStruct(field, BF16),
        (second, *halo),
        [pltpu.VMEM(field, F32), pltpu.VMEM(field, BF16), pltpu.SemaphoreType.DMA((4,))],
        out_space=pltpu.HBM,
    )


def exchange(top, bottom, left, right):
    grp = lax.axis_size("grp")
    tile = lax.axis_size("tile")
    up = [(i, (i + 1) % grp) for i in range(grp)]
    along = [(i, (i + 1) % tile) for i in range(tile)]
    above = lax.ppermute(bottom, "grp", up)
    below = lax.ppermute(top, "grp", [(b, a) for a, b in up])
    west = lax.ppermute(right, "tile", along)
    east = lax.ppermute(left, "tile", [(b, a) for a, b in along])
    return above, below, west, east


def on_device(temp, humid, parent, kabs, planck, top_flux):
    send, slot = pack(temp, humid, parent)
    recv = lax.all_to_all(send, "tile", split_axis=0, concat_axis=0, tiled=True)
    recv, halo = lax.optimization_barrier((recv, exchange(*edges(temp))))
    answer = owner_step(recv, kabs, planck, top_flux)
    answer, halo = lax.optimization_barrier((answer, halo))
    ret = lax.all_to_all(answer, "tile", split_axis=0, concat_axis=0, tiled=True)
    base, base_cols, slot_cols, hot, hot_cols = base_step(temp, humid, slot, halo)
    top, bottom, left, right = rim(ret, slot, slot_cols, base, base_cols, hot, hot_cols)
    halo = exchange(top, bottom, left, right)
    second = unpack(ret, slot, hot, base, top, bottom)
    return last_step(second, halo)


def solution(mesh):
    placed = (P(None, "grp", "tile"), P(None, "grp", "tile"), P("grp", "tile"), P(), P(), P())
    return jax.shard_map(
        on_device, mesh=mesh, in_specs=placed, out_specs=P(None, "grp", "tile"), check_vma=False
    )
```
